128 devices in a mesh: organ: 8 (over x, core), sub: 16 (over z, y).
Axes of the slice: x: 4, y: 4, z: 4, core: 2. Of those that a mesh axis runs over, the one named last changes fastest.
Arguments:
- dual_rhs: float32 [16, 8, 16, 5, 640], P(None, 'organ', 'sub')
- warm_start: float32 [16, 8, 16, 5, 640], P(None, 'organ', 'sub'), may hold values from -4 to 4
- inverse_blocks: float32 [8, 16, 5, 640, 640], P('organ', 'sub'), as said below
- coarse_basis: float32 [6, 8, 16, 5, 640], P(None, 'organ', 'sub')
- mortar_rows: float32 [8, 16, 512, 640], P('organ', 'sub'), may hold values from -0.25 to 0.25
- match_rounds: int32 [8, 16, 5], P('organ', 'sub'), may hold values from 0 to 4, each once within a row
- slave_owner: int32 [8, 16, 512, 1], P('organ', 'sub'), may hold values from 0 to 127; in each aligned block of 512 rows (0 to 511, 512 to 1023, ..., all dimensions but the last counted through in order) at most 8 rows name the same one
- slave_dofs: int32 [8, 16, 512], P('organ', 'sub'), may hold values from 0 to 639
- active_set: int32 [8, 16, 512], P('organ', 'sub'), may hold values 0 or 1
- row_counts: int32 [8, 16, 1], P('organ', 'sub'), may hold values from 384 to 512, as said below
Outputs:
- solution: float32 [16, 8, 16, 5, 640], P(None, 'organ', 'sub')
The draws below stay inside these ranges and needn't reach their ends.
Inputs may be any that keep to these rules, and one draw needn't show every extreme that they name: `match_rounds`: each device's row lists every round's face once. `slave_owner`: in the rows of one device no owner is named more than 8 times; in some device one owner is named exactly 8 times. `row_counts`: some device has all 512 rows live. `inverse_blocks`: each face block is symmetric positive definite.
All inputs are finite; a program needn't handle non-finite values. No bound on the sum of `active_set` on one device may be relied on, other than what follows from the above.
Results may differ from the reference program's by a relative error of at most 0.0001.
Values sent between devices are 32-bit elements; how exact they have to be, the bound alone decides.
A program may use at most 128 MiB of HBM per device.

```python
import math
import jax
import jax.numpy as jnp
import numpy as np
from jax import lax

NB = 640
DIRS = 16
ROUNDS = 5
MODES = 6
ITERS = 3
CAP = 8
BLOCKS = 5
ORGANS = 8
SUBS = 16
MROWS = 512


def draw_inverse_blocks(key, part):
    block_shape = (ORGANS, SUBS, BLOCKS, NB, NB)
    upper_part = jax.random.uniform(jax.random.fold_in(key, 1), block_shape, jnp.float32, -0.04, 0.04)
    positions = jnp.arange(NB)
    above = positions[:, None] < positions[None, :]
    mirrored = jnp.where(above, upper_part, jnp.swapaxes(upper_part, -1, -2))
    diag_vals = jax.random.uniform(jax.random.fold_in(key, 2), (ORGANS, SUBS, BLOCKS, NB), jnp.float32, 2.0, 3.0)
    diagonal_mask = positions[:, None] == positions[None, :]
    matrix = jnp.where(diagonal_mask, diag_vals[..., None], mirrored)
    return matrix


def coarse_and_load(key):
    mode_basis = jax.random.normal(jax.random.fold_in(key, 11), (MODES, ORGANS, SUBS, BLOCKS, NB), jnp.float32)
    weights = jax.random.normal(jax.random.fold_in(key, 12), (DIRS, ORGANS, MODES), jnp.float32) * 0.7
    rough_part = jax.random.normal(jax.random.fold_in(key, 13), (DIRS, ORGANS, SUBS, BLOCKS, NB), jnp.float32)
    loaded = rough_part
    for mode in range(MODES):
        loaded = loaded + weights[:, :, mode][:, :, None, None, None] * mode_basis[mode][None]
    position = jnp.arange(ORGANS * SUBS).reshape(ORGANS, SUBS).astype(jnp.float32)
    spread = 1.0 + 2.0 * position / max(ORGANS * SUBS - 1, 1)
    return (mode_basis, loaded * spread[None, :, :, None, None])


def draw_coarse_basis(key, part):
    return coarse_and_load(key)[0]


def draw_dual_rhs(key, part):
    return coarse_and_load(key)[1]


def draw_row_counts(key, part):
    device_total = ORGANS * SUBS
    counts = jax.random.randint(jax.random.fold_in(key, 21), (device_total,), 3 * MROWS // 4, MROWS + 1)
    full_device = jax.random.randint(jax.random.fold_in(key, 22), (), 0, device_total)
    counts = jnp.where(jnp.arange(device_total) == full_device, MROWS, counts)
    return counts.reshape(ORGANS, SUBS, 1).astype(jnp.int32)


def place_ends(drawn, rng, least, largest):
    longest = drawn.shape.index(max(drawn.shape))
    spots = []
    for shift in (0, 1):
        where = [jax.random.randint(jax.random.fold_in(rng, axis), (), 0, length) for axis, length in enumerate(drawn.shape)]
        where[longest] = (where[longest] + shift) % drawn.shape[longest]
        spots.append(tuple(where))
    return drawn.at[spots[0]].set(least).at[spots[1]].set(largest)


def level_of(key, shape, split, smallest, top_value):
    loudness, own = 1.0, jax.random.fold_in(key, 6)
    for dim, parts in split:
        heights = jnp.exp(jax.random.uniform(jax.random.fold_in(own, dim), (parts,), jnp.float32, smallest / len(split), top_value / len(split)))
        loudness = loudness * jnp.repeat(heights, shape[dim] // parts).reshape([-1 if axis == dim else 1 for axis in range(len(shape))])
    return loudness


def shared_out(rng, own, number, rows, count, top, bound, skew):
    order = jax.random.permutation(rng, count)
    packed, common = load_shares(count, rows * top, bound, skew, True), load_shares(count, rows * top, bound, skew, False)
    places = jnp.arange(count)

    def named(tallies, turn):
        used = int((tallies > 0).sum())
        fixed = max(1, used // 4)
        moved = fixed + (places - fixed + turn * (used - fixed)) % max(1, count - fixed)
        return jnp.zeros((count,), jnp.int32).at[order[jnp.where(places < fixed, places, moved)]].set(jnp.asarray(tallies, jnp.int32))

    tallies = jnp.where(number % 4 == 0, named(packed, number // 4), named(common, number - number // 4 - 1))
    mixed = jax.random.permutation(jax.random.fold_in(own, 3), count)
    donor, taker = mixed[0:count // 2 * 2:2], mixed[1:count // 2 * 2:2]
    margin = jnp.minimum(tallies[donor] - 1, bound - tallies[taker]) // 2
    margin = jnp.where((donor == order[0]) | (taker == order[0]) | (tallies[taker] == 0), 0, jnp.maximum(margin, 0))
    moved = jax.random.randint(jax.random.fold_in(own, 4), (count // 2,), 0, 1 << 20) % (margin + 1)
    tallies = tallies.at[donor].add(-moved).at[taker].add(moved)
    members = jnp.searchsorted(jnp.cumsum(tallies), jnp.arange(rows * top), side="right").astype(jnp.int32)
    grid = members.reshape(top, rows).T
    grid = grid[jax.random.permutation(jax.random.fold_in(own, 1), rows)]
    turn = jax.random.randint(jax.random.fold_in(own, 2), (rows, 1), 0, top)
    return jnp.take_along_axis(grid, (jnp.arange(top)[None, :] + turn) % top, axis=1)


def load_shares(count, total, limit, slope, full):
    loads = [(1 << 20) // math.isqrt(standing ** slope) + 1 for standing in range(1, count + 1)]
    largest = limit if full else min(limit, max(-(-total // count), total * loads[0] // sum(loads)))
    least = 1 if total - largest >= count - 1 else 0
    holding, spare = [largest] + [least] * (count - 1), total - largest - least * (count - 1)
    while spare > 0:
        free = [i for i in range(1, count) if holding[i] < largest] or [i for i in range(1, count) if holding[i] < limit]
        whole, budget = sum([loads[i] for i in free]), spare
        for i in free:
            addition = min(limit - holding[i], max(1, budget * loads[i] // whole), spare)
            holding[i] = holding[i] + addition
            spare = spare - addition
    return np.array(holding)


def centred(rng, dims, width, bound, shards=(), kind=jnp.bfloat16):
    values = width * jax.random.normal(rng, dims, jnp.float32)
    if shards:
        values = values * level_of(rng, dims, shards, -0.22, 0.18)
    return jnp.clip(values, -bound, bound).astype(kind)


def setup_inputs(seed: int = 0) -> dict:
    key_list = jax.random.split(jax.random.key(seed), 11)
    dual_rhs = draw_dual_rhs(jax.random.fold_in(key_list[10], 71), 0)
    warm_start = centred(key_list[1], (DIRS, ORGANS, SUBS, BLOCKS, NB), 0.3, 4.0, ((1, 8), (2, 16)), jnp.float32)
    inverse_blocks = draw_inverse_blocks(jax.random.fold_in(key_list[10], 71), 0)
    coarse_basis = draw_coarse_basis(jax.random.fold_in(key_list[10], 71), 0)
    mortar_rows = centred(key_list[4], (ORGANS, SUBS, MROWS, NB), NB ** -0.5, 0.25, ((0, 8), (1, 16)), jnp.float32)
    match_rounds = jax.vmap(lambda own: jax.random.permutation(own, ROUNDS))(jax.random.split(key_list[5], ORGANS * SUBS)).reshape((ORGANS, SUBS, ROUNDS)).astype(jnp.int32)
    slave_owner_keys = jax.random.split(jax.random.fold_in(key_list[6], 1), ORGANS * SUBS * MROWS // MROWS)
    slave_owner_turns = jax.random.permutation(jax.random.fold_in(key_list[6], 3), ORGANS * SUBS * MROWS // MROWS)
    slave_owner = jax.vmap(lambda own, number: shared_out(jax.random.fold_in(key_list[6], 2), own, number, MROWS, ORGANS * SUBS, 1, CAP, 2))(slave_owner_keys, slave_owner_turns).reshape((ORGANS, SUBS, MROWS, 1))
    slave_dofs = place_ends(jax.random.randint(key_list[7], (ORGANS, SUBS, MROWS), 0, NB), jax.random.fold_in(key_list[7], 1), 0, NB - 1).astype(jnp.int32)
    active_set = place_ends((jax.random.randint(key_list[8], (ORGANS, SUBS, MROWS), 0, 8) < 7).astype(jnp.int32), jax.random.fold_in(key_list[8], 1), 0, 1)
    row_counts = draw_row_counts(jax.random.fold_in(key_list[10], 71), 0)
    return {"dual_rhs": dual_rhs, "warm_start": warm_start, "inverse_blocks": inverse_blocks, "coarse_basis": coarse_basis, "mortar_rows": mortar_rows, "match_rounds": match_rounds, "slave_owner": slave_owner, "slave_dofs": slave_dofs, "active_set": active_set, "row_counts": row_counts}


def apply_jump(field, match_rounds, mortar_rows, flat_index, live_rows):
    result = field
    block_ids = jnp.arange(BLOCKS, dtype=jnp.int32)
    for round_index in range(ROUNDS):
        selector = (match_rounds[:, :, round_index][:, :, None] == block_ids[None, None, :]).astype(jnp.float32)
        face_vals = jnp.sum(selector[None, :, :, :, None] * field, axis=3)
        if round_index < 3:
            partner = jnp.bitwise_xor(jnp.arange(SUBS, dtype=jnp.int32), 1 << round_index)
            remote = face_vals[:, :, partner, :]
        else:
            partner = jnp.bitwise_xor(jnp.arange(ORGANS, dtype=jnp.int32), 1 << round_index - 3)
            remote = face_vals[:, partner, :, :]
        result = result - selector[None, :, :, :, None] * remote[:, :, :, None, :]
    surface = field[:, :, :, 0, :]
    row_vals = jnp.einsum('kosn,osrn->kosr', surface, mortar_rows, precision=lax.Precision.HIGHEST)
    flat_surface = surface.reshape(DIRS, ORGANS * SUBS * NB)
    slave_vals = flat_surface[:, flat_index]
    gap_vals = live_rows[None] * (row_vals - slave_vals)
    master_part = jnp.einsum('kosr,osrn->kosn', gap_vals, mortar_rows, precision=lax.Precision.HIGHEST)
    slave_part = jnp.zeros((DIRS, ORGANS * SUBS * NB), jnp.float32).at[:, flat_index.reshape(-1)].add(gap_vals.reshape(DIRS, -1))
    slave_part = slave_part.reshape(DIRS, ORGANS, SUBS, NB)
    return result.at[:, :, :, 0, :].add(master_part - slave_part)

def reference(dual_rhs, warm_start, inverse_blocks, coarse_basis, mortar_rows, match_rounds, slave_owner, slave_dofs, active_set, row_counts):
    positions = jnp.arange(MROWS, dtype=jnp.int32)
    live_rows = (active_set * (positions[None, None, :] < row_counts).astype(jnp.int32)).astype(jnp.float32)
    flat_index = (slave_owner[:, :, :, 0] * NB + slave_dofs).astype(jnp.int32)

    def jump(field):
        return apply_jump(field, match_rounds, mortar_rows, flat_index, live_rows)

    def operator(field):
        inner = jump(field)
        smoothed = jnp.einsum('kosbn,osbnm->kosbm', inner, inverse_blocks, precision=lax.Precision.HIGHEST)
        return jump(smoothed)
    gram_matrix = jnp.einsum('mosbn,losbn->oml', coarse_basis, coarse_basis, precision=lax.Precision.HIGHEST)
    factors = [jnp.linalg.cholesky(gram_matrix[organ]) for organ in range(ORGANS)]

    def project(resid):
        coeffs = jnp.einsum('kosbn,mosbn->kom', resid, coarse_basis, precision=lax.Precision.HIGHEST)
        solved = jnp.stack([jax.scipy.linalg.cho_solve((factors[organ], True), coeffs[:, organ, :].T).T for organ in range(ORGANS)], axis=1)
        return resid - jnp.einsum('kom,mosbn->kosbn', solved, coarse_basis, precision=lax.Precision.HIGHEST)
    solution = warm_start
    resid = dual_rhs - operator(warm_start)
    projected = project(resid)
    direction = projected
    rho_now = jnp.sum(resid * projected, axis=(1, 2, 3, 4))
    for iteration in range(ITERS):
        image = operator(direction)
        step_size = rho_now / jnp.sum(direction * image, axis=(1, 2, 3, 4))
        solution = solution + step_size[:, None, None, None, None] * direction
        if iteration < ITERS - 1:
            resid = resid - step_size[:, None, None, None, None] * image
            projected = project(resid)
            rho_new = jnp.sum(resid * projected, axis=(1, 2, 3, 4))
            direction = projected + (rho_new / rho_now)[:, None, None, None, None] * direction
            rho_now = rho_new
    return solution
```

```python
import jax
import jax.numpy as jnp
from jax import lax
from jax.experimental import pallas as pl
from jax.experimental.pallas import tpu as pltpu
from jax.sharding import PartitionSpec as P

ITERS = 3
CAP = 8
MESH = pl.DeviceIdType.MESH
F32 = jnp.float32
BF16 = jnp.bfloat16
N_ORG, N_SUB = 8, 16
N_DEV = N_ORG * N_SUB
LANES = 128
ROWS = (1, 4, 3, 3, 3, 3, 3, 3, 1)
N_ROUND = len(ROWS)
N_MATCH = 5
N_HALO = 2 * ITERS + 1


def iota(shape, dim):
    return lax.broadcasted_iota(jnp.int32, shape, dim)


def split3(x):
    high = x.astype(BF16)
    rest = x - high.astype(F32)
    mid = rest.astype(BF16)
    low = (rest - mid.astype(F32)).astype(BF16)
    return high, mid, low


def split2(x):
    high = x.astype(BF16)
    return high, (x - high.astype(F32)).astype(BF16)


def dot(a, b):
    return jnp.dot(a, b, preferred_element_type=F32)


def mm(x, w_high, w_low):
    n = x.shape[0]
    high, mid, low = split3(x)
    a = dot(jnp.concatenate([high, mid, low], axis=0), w_high)
    b = dot(jnp.concatenate([high, mid], axis=0), w_low)
    return a[:n] + (a[n : 2 * n] + b[:n] + (a[2 * n :] + b[n:]))


def offset_of(u):
    return u - (u // 2) * (2 * u - 5)


def kernel(
    rhs_hbm,
    warm_hbm,
    inv_hbm,
    coarse_hbm,
    mortar_hbm,
    owner_ref,
    dofs_ref,
    active_ref,
    rounds_ref,
    counts_ref,
    out_hbm,
    g_stage,
    g_high,
    g_low,
    m_stage,
    pick_ref,
    wf_high,
    wf_low,
    wb_high,
    wb_low,
    wt_high,
    wt_low,
    q_ref,
    qt_ref,
    p_ref,
    d_ref,
    w_ref,
    y_ref,
    yp_ref,
    ym_ref,
    r_ref,
    sol_ref,
    q_stage,
    x_stage,
    r_stage,
    msend,
    qsend,
    qrecv,
    *rest,
):
    sends, recvs = rest[:N_ROUND], rest[N_ROUND : 2 * N_ROUND]
    mrecv = rest[2 * N_ROUND : 2 * N_ROUND + N_HALO]
    (load_sem, out_sem, send_sem, recv_sem, self_sem, ms_sem, mr_sem, qs_sem, qr_sem) = rest[
        2 * N_ROUND + N_HALO :
    ]
    faces, dirs, length = p_ref.shape
    rows = m_stage.shape[0]
    modes = coarse_hbm.shape[0]
    slots = CAP * N_DEV
    org, sub = lax.axis_index("organ"), lax.axis_index("sub")
    me = org * N_SUB + sub
    x_at, core_at, z_at, y_at = org // 2, org % 2, sub // 4, sub % 4

    def peer(i):
        u = N_DEV - 1 - i
        px = (x_at + offset_of(u // 32)) % 4
        pc = (core_at + (u // 16) % 2) % 2
        pz = (z_at + offset_of((u // 4) % 4)) % 4
        py = (y_at + offset_of(u % 4)) % 4
        return px * 2 + pc, pz * 4 + py

    barrier = pltpu.get_barrier_semaphore()

    def greet(i, carry):
        pl.semaphore_signal(barrier, inc=1, device_id=peer(i), device_id_type=MESH)
        return carry

    lax.fori_loop(0, N_DEV - 1, greet, 0)

    loads = [pltpu.make_async_copy(mortar_hbm, m_stage, load_sem.at[0])]
    q_ref[...] = jnp.zeros(q_ref.shape, F32)
    qt_ref[...] = jnp.zeros(qt_ref.shape, F32)
    q_loads = [pltpu.make_async_copy(coarse_hbm, q_stage, load_sem.at[1])]
    x_loads = [pltpu.make_async_copy(warm_hbm, x_stage, load_sem.at[6])]
    r_loads = [pltpu.make_async_copy(rhs_hbm, r_stage, load_sem.at[11])]
    g_loads = [
        pltpu.make_async_copy(inv_hbm.at[f], g_stage.at[f], load_sem.at[16 + f])
        for f in range(faces)
    ]
    for copy in loads + q_loads + x_loads + r_loads + g_loads:
        copy.start()

    def start_round(i):
        n = ROWS[i]
        sb, rb = sends[i], recvs[i]

        def go(step, carry):
            po, ps = peer(step)
            pltpu.make_async_remote_copy(
                sb.at[pl.ds((po * N_SUB + ps) * n, n)],
                rb.at[pl.ds(me * n, n)],
                send_sem.at[i],
                recv_sem.at[i],
                device_id=(po, ps),
                device_id_type=MESH,
            ).start()
            return carry

        lax.fori_loop(0, N_DEV - 1, go, 0)
        pltpu.make_async_copy(
            sb.at[pl.ds(me * n, n)], rb.at[pl.ds(me * n, n)], self_sem.at[i]
        ).start()

    def wait_round(i):
        n = ROWS[i]
        sb, rb = sends[i], recvs[i]
        pltpu.make_async_copy(
            sb.at[pl.ds(me * n, n)], rb.at[pl.ds(me * n, n)], self_sem.at[i]
        ).wait()
        most = pl.ds(0, (N_DEV - 1) * n)
        pltpu.make_async_copy(rb.at[most], rb.at[most], recv_sem.at[i]).wait()
        pltpu.make_async_copy(sb.at[most], sb.at[most], send_sem.at[i]).wait()

    def put(i, j, value):
        sends[i][pl.ds(j, N_DEV, stride=ROWS[i]), :] = value

    def got(i, j):
        return recvs[i][pl.ds(j, N_DEV, stride=ROWS[i]), :]

    def partners():
        out = []
        for r in range(3):
            step = 2**r
            out.append((org, sub + step * (1 - 2 * ((sub // step) % 2))))
        for r in range(2):
            step = 2**r
            out.append((org + step * (1 - 2 * ((org // step) % 2)), sub))
        return out

    face_of = [rounds_ref[0, r] for r in range(N_MATCH)]
    round_of = []
    for f in range(faces):
        found = jnp.int32(0)
        for r in range(1, N_MATCH):
            found = jnp.where(face_of[r] == f, r, found)
        round_of.append(found)

    def start_match(source, send, recv, s_sem, r_sem):
        copies = []
        for r, dev in enumerate(partners()):
            send[r] = source[face_of[r]]
        for r, dev in enumerate(partners()):
            copy = pltpu.make_async_remote_copy(
                send.at[r], recv.at[r], s_sem.at[r], r_sem.at[r], device_id=dev, device_id_type=MESH
            )
            copy.start()
            copies.append(copy)
        return copies

    live = (active_ref[...] > 0) & (iota((1, rows), 1) < counts_ref[0, 0])
    owner = jnp.where(live, owner_ref[...], -1)
    owned = iota((N_DEV, rows), 0) == owner
    before = (iota((rows, rows), 0) < iota((rows, rows), 1)).astype(F32).astype(BF16)
    earlier = dot(owned.astype(F32).astype(BF16), before)
    rank = jnp.sum(jnp.where(owned, earlier, 0.0), axis=0, keepdims=True).astype(jnp.int32)
    slot = jnp.where(live, rank * N_DEV + owner, -1)
    dof_plus = dofs_ref[...].astype(F32) + 1.0
    lane = iota((N_DEV, LANES), 1)
    table = jnp.zeros((N_DEV, LANES), F32)
    for k in range(CAP):
        chosen = iota((N_DEV, rows), 0) + k * N_DEV == slot
        pick_ref[k] = chosen.astype(F32).astype(BF16)
        column = jnp.sum(jnp.where(chosen, dof_plus, 0.0), axis=1, keepdims=True) - 1.0
        table = jnp.where(lane == k, column, table)

    for copy in q_loads:
        copy.wait()
    for f in range(faces):
        q_ref[f, :modes] = q_stage[:, f, :]
    gram = jnp.zeros((8, LANES), F32)
    for f in range(faces):
        own = q_ref[f, :8]
        tiled = jnp.concatenate([own] * (LANES // 8), axis=0)
        gram = gram + lax.dot_general(
            own, tiled, (((1,), (1,)), ((), ())), precision=lax.Precision.HIGHEST,
            preferred_element_type=F32,
        )
    keep = iota((8, LANES), 1) // 8 == iota((8, LANES), 0) + 8
    table = table + jnp.sum(jnp.where(keep, gram, 0.0), axis=0, keepdims=True)
    put(0, 0, table)
    pl.semaphore_wait(barrier, N_DEV - 1)
    start_round(0)

    for copy in loads:
        copy.wait()
    m_high, m_low = split2(m_stage[...])

    def arrange(k, carry):
        at = pl.ds(pl.multiple_of(k * N_DEV, N_DEV), N_DEV)
        for part, back, ahead in ((m_high, wb_high, wf_high), (m_low, wb_low, wf_low)):
            block = dot(pick_ref[k], part)
            back[at, :] = block.astype(BF16)
            ahead[:, at] = block.T.astype(BF16)
        return carry

    lax.fori_loop(0, CAP, arrange, 0)

    eye = [iota((dirs, LANES), 1) == iota((dirs, LANES), 0) + dirs * m for m in range(8)]

    def to_row(columns):
        total = jnp.zeros((dirs, LANES), F32)
        for m, column in columns:
            total = total + jnp.where(eye[m], column, 0.0)
        return jnp.sum(total, axis=0, keepdims=True)

    def to_column(row, m):
        return jnp.sum(jnp.where(eye[m], row, 0.0), axis=1, keepdims=True)

    def inner(a_ref, b_ref):
        total = a_ref[0] * b_ref[0]
        for f in range(1, faces):
            total = total + a_ref[f] * b_ref[f]
        return jnp.sum(total, axis=1, keepdims=True)

    for copy in r_loads:
        copy.wait()
    for f in range(faces):
        r_ref[f] = r_stage[:, f, :]
    rhs_modes = []
    for m in range(modes):
        total = r_ref[0] * q_ref[0, m : m + 1]
        for f in range(1, faces):
            total = total + r_ref[f] * q_ref[f, m : m + 1]
        rhs_modes.append((m, jnp.sum(total, axis=1, keepdims=True)))
    rhs_row = to_row(rhs_modes)

    for copy in x_loads:
        copy.wait()
    for f in range(faces):
        p_ref[f] = x_stage[:, f, :]
    copies = start_match(p_ref, msend.at[0], mrecv[0], ms_sem.at[0], mr_sem.at[0])
    for r in range(N_MATCH):
        qsend[r] = q_ref[face_of[r], :8]
    q_copies = []
    for r, dev in enumerate(partners()):
        copy = pltpu.make_async_remote_copy(
            qsend.at[r], qrecv.at[r], qs_sem.at[r], qr_sem.at[r], device_id=dev, device_id_type=MESH
        )
        copy.start()
        q_copies.append(copy)

    wait_round(0)
    table = recvs[0][...]
    table_t = table.T
    in_group = iota((N_DEV, LANES), 0) // N_SUB == org
    gram_row = jnp.sum(jnp.where(in_group, table, 0.0), axis=0, keepdims=True)
    for k in range(CAP):
        column = table[:, k : k + 1].astype(jnp.int32)
        hit = iota((N_DEV, length), 1) == column
        wb_high[slots + k * N_DEV : slots + (k + 1) * N_DEV, :] = jnp.where(hit, -1.0, 0.0).astype(BF16)
        hit = iota((length, N_DEV), 0) == table_t[k : k + 1, :].astype(jnp.int32)
        wf_high[:, slots + k * N_DEV : slots + (k + 1) * N_DEV] = jnp.where(hit, 1.0, 0.0).astype(BF16)

    def row_values(x):
        n = x.shape[0]
        high, mid, low = split3(x)
        full = dot(jnp.concatenate([high, mid, low], axis=0), wf_high[...])
        fine = dot(jnp.concatenate([high, mid], axis=0), wf_low[...])
        full = full[:n] + (full[n : 2 * n] + full[2 * n :])
        return full[:, :slots] + (fine[:n] + fine[n:]), full[:, slots:]

    def spread_gaps(gaps):
        n = gaps.shape[0]
        high, mid, low = split3(gaps)
        full = dot(jnp.concatenate([high, mid, low], axis=0), wb_high[...])
        fine = dot(jnp.concatenate([high[:, :slots], mid[:, :slots]], axis=0), wb_low[...])
        return full[:n] + (full[n : 2 * n] + fine[:n] + (full[2 * n :] + fine[n:]))

    def stacked(value):
        return jnp.concatenate(
            [value[:, k * N_DEV : (k + 1) * N_DEV] for k in range(CAP)], axis=0
        )

    def unstacked(value):
        n = value.shape[0] // CAP
        return jnp.concatenate([value[k * n : (k + 1) * n] for k in range(CAP)], axis=1)

    def face_gaps(i, mine_a, mine_s):
        theirs_a, theirs_s = got(i, 0).T, got(i, 1).T
        return jnp.concatenate(
            [unstacked(mine_a - theirs_s), unstacked(theirs_a - mine_s)], axis=1
        )

    both_a, both_s = row_values(jnp.concatenate([p_ref[0], q_ref[0]], axis=0))
    mine_a, mine_s = stacked(both_a[:dirs]), stacked(both_s[:dirs])
    qa, qs = both_a[dirs : dirs + 8], both_s[dirs : dirs + 8]
    put(1, 0, mine_a.T)
    put(1, 1, mine_s.T)
    put(1, 2, jnp.broadcast_to(rhs_row, (N_DEV, LANES)))
    put(1, 3, jnp.concatenate([stacked(qa), stacked(qs)], axis=0).T)
    start_round(1)

    def gram_at(i, j):
        at = 64 + 8 * i + j
        return gram_row[:, at : at + 1]

    factor, inverse = {}, []
    for j in range(modes):
        pivot = gram_at(j, j)
        for k in range(j):
            pivot = pivot - factor[j, k] * factor[j, k]
        pivot = jnp.sqrt(pivot)
        inverse.append(1.0 / pivot)
        for i in range(j + 1, modes):
            value = gram_at(i, j)
            for k in range(j):
                value = value - factor[i, k] * factor[j, k]
            factor[i, j] = value * inverse[j]
    for f in range(faces):
        made = []
        for i in range(modes):
            row = q_ref[f, i : i + 1]
            for k in range(i):
                row = row - factor[i, k] * made[k]
            made.append(row * inverse[i])
            qt_ref[f, i : i + 1] = made[i]

    chunk = 64
    for f in range(faces):
        g_loads[f].wait()

        def halve(i, carry, f=f):
            at = pl.ds(pl.multiple_of(i * chunk, chunk), chunk)
            high, low = split2(g_stage[f, at, :])
            g_high[f, at, :] = high
            g_low[f, at, :] = low
            return carry

        lax.fori_loop(0, length // chunk, halve, 0)

    rho = None
    c_res = None
    for t in range(ITERS + 1):
        a_round = 1 + 2 * t
        for copy in copies:
            copy.wait()
        halo = mrecv[2 * t]
        for f in range(faces):
            yp_ref[f] = p_ref[f] - halo[round_of[f]]

        def smooth_face(f, carry):
            ym_ref[f] = mm(
                yp_ref[f], g_high[f], g_low[f]
            )
            return carry

        lax.fori_loop(1, faces, smooth_face, 0)

        wait_round(a_round)
        gaps = face_gaps(a_round, mine_a, mine_s)
        if t == 0:
            for copy in q_copies:
                copy.wait()
            c_row = jnp.sum(jnp.where(in_group, got(1, 2), 0.0), axis=0, keepdims=True)
            c_res = [to_column(c_row, m) for m in range(modes)]
            theirs = got(1, 3).T
            organ_row = iota((8, LANES), 0)
            of_peer = iota((8, LANES), 1) // N_SUB == organ_row
            mine = organ_row == org
            blocks = []
            for m in range(modes):
                outs, ins = [], []
                for k in range(CAP):
                    at = slice(k * N_DEV, (k + 1) * N_DEV)
                    ta = theirs[k * 8 + m : k * 8 + m + 1]
                    ts = theirs[64 + k * 8 + m : 64 + k * 8 + m + 1]
                    outs.append(
                        jnp.where(mine, qa[m : m + 1, at], 0.0) - jnp.where(of_peer, ts, 0.0)
                    )
                    ins.append(
                        jnp.where(of_peer, ta, 0.0) - jnp.where(mine, qs[m : m + 1, at], 0.0)
                    )
                blocks.append(jnp.concatenate(outs + ins, axis=1))
            mode_gaps = jnp.concatenate(blocks, axis=0)
            both = spread_gaps(jnp.concatenate([gaps, mode_gaps], axis=0))
            contact, mode_contact = both[:dirs], both[dirs:]
            organ_col = iota((8, length), 0)
            for f in range(faces):
                at_round = round_of[f]
                other = jnp.where(
                    at_round < 3,
                    org,
                    jnp.where(
                        at_round == 3, org + 1 - 2 * (org % 2), org + 2 - 4 * ((org // 2) % 2)
                    ),
                )
                arrived = qrecv[at_round]
                parts = []
                for m in range(modes):
                    part = jnp.where(organ_col == org, q_ref[f, m : m + 1], 0.0) - jnp.where(
                        organ_col == other, arrived[m : m + 1], 0.0
                    )
                    if f == 0:
                        part = part + mode_contact[8 * m : 8 * m + 8]
                    parts.append(part)
                parts.append(jnp.zeros((LANES - 8 * modes, length), F32))
                wide = jnp.concatenate(parts, axis=0).T
                high, low = split2(wide)
                wt_high[f] = high
                wt_low[f] = low
        else:
            contact = spread_gaps(gaps)
            rho_new = to_column(jnp.sum(got(a_round, 2), axis=0, keepdims=True), 0)
            beta = rho_new / rho if t > 1 else None
            rho = rho_new
        yp_ref[0] = yp_ref[0] + contact
        ym_ref[0] = mm(yp_ref[0], g_high[0], g_low[0])

        for f in range(faces):
            made = ym_ref[f]
            if t > 1:
                w_ref[f] = yp_ref[f] + beta * w_ref[f]
                y_ref[f] = made + beta * y_ref[f]
                d_ref[f] = p_ref[f] + beta * d_ref[f]
            else:
                w_ref[f] = yp_ref[f]
                y_ref[f] = made
                d_ref[f] = p_ref[f]
        curved = inner(w_ref, y_ref)

        b_round = a_round + 1
        if t == ITERS:
            put(b_round, 0, jnp.broadcast_to(to_row([(0, curved)]), (N_DEV, LANES)))
            start_round(b_round)
            wait_round(b_round)
            step = rho / to_column(jnp.sum(recvs[b_round][...], axis=0, keepdims=True), 0)
            for f in range(faces):
                sol_ref[f] = sol_ref[f] + step * d_ref[f]
            break

        copies = start_match(
            y_ref, msend.at[2 * t + 1], mrecv[2 * t + 1], ms_sem.at[2 * t + 1], mr_sem.at[2 * t + 1]
        )
        mine_a, mine_s = row_values(y_ref[0])
        mine_a, mine_s = stacked(mine_a), stacked(mine_s)
        put(b_round, 0, mine_a.T)
        put(b_round, 1, mine_s.T)
        coarse = mm(y_ref[0], wt_high[0], wt_low[0])
        for f in range(1, faces):
            coarse = coarse + mm(y_ref[f], wt_high[f], wt_low[f])
        coarse = jnp.concatenate([coarse, jnp.zeros((LANES - dirs, LANES), F32)], axis=0).T
        parts = [coarse[8 * m : 8 * m + 8, :dirs] for m in range(modes)]
        parts.append(jnp.zeros((8, LANES - modes * dirs), F32))
        coarse = jnp.concatenate(parts, axis=1) + to_row([(modes, curved)])
        for o in range(N_ORG):
            sends[b_round][pl.ds(o * N_SUB * ROWS[b_round] + 2, N_SUB, stride=ROWS[b_round]), :] = (
                jnp.broadcast_to(coarse[o : o + 1], (N_SUB, LANES))
            )
        start_round(b_round)

        for copy in copies:
            copy.wait()
        halo = mrecv[2 * t + 1]
        for f in range(faces):
            yp_ref[f] = y_ref[f] - halo[round_of[f]]
        wait_round(b_round)
        yp_ref[0] = yp_ref[0] + spread_gaps(face_gaps(b_round, mine_a, mine_s))
        total = jnp.sum(got(b_round, 2), axis=0, keepdims=True)
        c_image = [to_column(total, m) for m in range(modes)]
        if t > 0:
            step = rho / to_column(total, modes)
        for f in range(faces):
            if t > 0:
                sol_ref[f] = sol_ref[f] + step * d_ref[f]
                r_ref[f] = r_ref[f] - step * yp_ref[f]
            else:
                sol_ref[f] = d_ref[f]
                r_ref[f] = r_ref[f] - yp_ref[f]
        for m in range(modes):
            c_res[m] = c_res[m] - (step * c_image[m] if t > 0 else c_image[m])
        solved = []
        for i in range(modes):
            value = c_res[i]
            for k in range(i):
                value = value - factor[i, k] * solved[k]
            solved.append(value * inverse[i])
        for f in range(faces):
            value = r_ref[f]
            for m in range(modes):
                value = value - solved[m] * qt_ref[f, m : m + 1]
            p_ref[f] = value

        n_halo = 2 * t + 2
        copies = start_match(
            p_ref, msend.at[n_halo], mrecv[n_halo], ms_sem.at[n_halo], mr_sem.at[n_halo]
        )
        mine_a, mine_s = row_values(p_ref[0])
        mine_a, mine_s = stacked(mine_a), stacked(mine_s)
        put(b_round + 1, 0, mine_a.T)
        put(b_round + 1, 1, mine_s.T)
        put(
            b_round + 1,
            2,
            jnp.broadcast_to(to_row([(0, inner(r_ref, p_ref))]), (N_DEV, LANES)),
        )
        start_round(b_round + 1)

    for f in range(faces):
        x_stage[:, f, :] = sol_ref[f]
    write = pltpu.make_async_copy(x_stage, out_hbm, out_sem.at[0])
    write.start()
    write.wait()


def local(
    dual_rhs,
    warm_start,
    inverse_blocks,
    coarse_basis,
    mortar_rows,
    match_rounds,
    slave_owner,
    slave_dofs,
    active_set,
    row_counts,
):
    dirs, _, _, faces, length = dual_rhs.shape
    rows = mortar_rows.shape[2]
    modes = coarse_basis.shape[0]
    slots = CAP * N_DEV
    field = pltpu.VMEM((faces, dirs, length), F32)
    dma = pltpu.SemaphoreType.DMA
    any_spec = pl.BlockSpec(memory_space=pl.ANY)
    vmem_spec = pl.BlockSpec(memory_space=pltpu.VMEM)
    smem_spec = pl.BlockSpec(memory_space=pltpu.SMEM)
    scratch = [
        pltpu.VMEM((faces, length, length), F32),
        pltpu.VMEM((faces, length, length), BF16),
        pltpu.VMEM((faces, length, length), BF16),
        pltpu.VMEM((rows, length), F32),
        pltpu.VMEM((CAP, N_DEV, rows), BF16),
        pltpu.VMEM((length, 2 * slots), BF16),
        pltpu.VMEM((length, slots), BF16),
        pltpu.VMEM((2 * slots, length), BF16),
        pltpu.VMEM((slots, length), BF16),
        pltpu.VMEM((faces, length, LANES), BF16),
        pltpu.VMEM((faces, length, LANES), BF16),
        field,
        pltpu.VMEM((faces, 8, length), F32),
    ]
    scratch += [field] * 8
    scratch += [
        pltpu.VMEM((modes, faces, length), F32),
        pltpu.VMEM((dirs, faces, length), F32),
        pltpu.VMEM((dirs, faces, length), F32),
        pltpu.VMEM((N_HALO, N_MATCH, dirs, length), F32),
        pltpu.VMEM((N_MATCH, 8, length), F32),
        pltpu.VMEM((N_MATCH, 8, length), F32),
    ]
    scratch += [pltpu.VMEM((N_DEV * n, LANES), F32) for n in ROWS] * 2
    scratch += [pltpu.VMEM((N_MATCH, dirs, length), F32)] * N_HALO
    scratch += [
        dma((21,)),
        dma((faces,)),
        dma((N_ROUND,)),
        dma((N_ROUND,)),
        dma((N_ROUND,)),
        dma((N_HALO, N_MATCH)),
        dma((N_HALO, N_MATCH)),
        dma((N_MATCH,)),
        dma((N_MATCH,)),
    ]
    result = pl.pallas_call(
        kernel,
        out_shape=jax.ShapeDtypeStruct((dirs, faces, length), F32),
        in_specs=[any_spec] * 5 + [vmem_spec] * 3 + [smem_spec] * 2,
        out_specs=any_spec,
        scratch_shapes=scratch,
        compiler_params=pltpu.CompilerParams(
            collective_id=0, has_side_effects=True, vmem_limit_bytes=60 * 2**20
        ),
    )(
        dual_rhs.reshape(dirs, faces, length),
        warm_start.reshape(dirs, faces, length),
        inverse_blocks.reshape(faces, length, length),
        coarse_basis.reshape(modes, faces, length),
        mortar_rows.reshape(rows, length),
        slave_owner.reshape(1, rows),
        slave_dofs.reshape(1, rows),
        active_set.reshape(1, rows),
        match_rounds.reshape(1, N_MATCH),
        row_counts.reshape(1, 1),
    )
    return result.reshape(dirs, 1, 1, faces, length)


def solution(mesh):
    in_specs = (
        P(None, "organ", "sub", None, None),
        P(None, "organ", "sub", None, None),
        P("organ", "sub", None, None, None),
        P(None, "organ", "sub", None, None),
        P("organ", "sub", None, None),
        P("organ", "sub", None),
        P("organ", "sub", None, None),
        P("organ", "sub", None),
        P("organ", "sub", None),
        P("organ", "sub", None),
    )
    out_specs = P(None, "organ", "sub", None, None)
    return jax.shard_map(local, mesh=mesh, in_specs=in_specs, out_specs=out_specs, check_vma=False)
```

```python
import jax
import jax.numpy as jnp
from jax import lax
from jax.experimental import pallas as pl
from jax.experimental.pallas import tpu as pltpu
from jax.sharding import PartitionSpec as P

ITERS = 3
CAP = 8
MESH = pl.DeviceIdType.MESH
F32 = jnp.float32
BF16 = jnp.bfloat16
N_ORG, N_SUB = 8, 16
N_DEV = N_ORG * N_SUB
LANES = 128
ROWS = (1, 4, 3, 3, 3, 3, 3, 3, 1)
N_ROUND = len(ROWS)
N_MATCH = 5
N_HALO = 2 * ITERS + 1


def iota(shape, dim):
    return lax.broadcasted_iota(jnp.int32, shape, dim)


def split3(x):
    high = x.astype(BF16)
    rest = x - high.astype(F32)
    mid = rest.astype(BF16)
    low = (rest - mid.astype(F32)).astype(BF16)
    return high, mid, low


def split2(x):
    high = x.astype(BF16)
    return high, (x - high.astype(F32)).astype(BF16)


def dot(a, b):
    return jnp.dot(a, b, preferred_element_type=F32)


def mm(x, w_high, w_low):
    n = x.shape[0]
    high, mid, low = split3(x)
    a = dot(jnp.concatenate([high, mid, low], axis=0), w_high)
    b = dot(jnp.concatenate([high, mid], axis=0), w_low)
    return a[:n] + (a[n : 2 * n] + b[:n] + (a[2 * n :] + b[n:]))


def offset_of(u):
    return u - (u // 2) * (2 * u - 5)


def kernel(
    rhs_hbm,
    warm_hbm,
    inv_hbm,
    coarse_hbm,
    mortar_hbm,
    owner_ref,
    dofs_ref,
    active_ref,
    rounds_ref,
    counts_ref,
    out_hbm,
    g_stage,
    g_high,
    g_low,
    m_stage,
    pick_ref,
    wf_high,
    wf_low,
    wb_high,
    wb_low,
    wt_high,
    wt_low,
    q_ref,
    qt_ref,
    p_ref,
    d_ref,
    w_ref,
    y_ref,
    yp_ref,
    ym_ref,
    r_ref,
    sol_ref,
    q_stage,
    x_stage,
    r_stage,
    msend,
    qsend,
    qrecv,
    *rest,
):
    sends, recvs = rest[:N_ROUND], rest[N_ROUND : 2 * N_ROUND]
    mrecv = rest[2 * N_ROUND : 2 * N_ROUND + N_HALO]
    (load_sem, out_sem, send_sem, recv_sem, self_sem, ms_sem, mr_sem, qs_sem, qr_sem) = rest[
        2 * N_ROUND + N_HALO :
    ]
    faces, dirs, length = p_ref.shape
    rows = m_stage.shape[0]
    modes = coarse_hbm.shape[0]
    slots = CAP * N_DEV
    org, sub = lax.axis_index("organ"), lax.axis_index("sub")
    me = org * N_SUB + sub
    x_at, core_at, z_at, y_at = org // 2, org % 2, sub // 4, sub % 4

    organs = [
        ((x_at + dx) % 4) * 2 + (core_at + dc) % 2 for dx in (2, 3, 1, 0) for dc in (1, 0)
    ]

    def each_peer(visit):
        def subs(i, carry):
            z_to = (z_at + offset_of(3 - i // 4)) % 4
            y_to = (y_at + offset_of(3 - i % 4)) % 4
            for o in organs:
                visit(o, z_to * 4 + y_to)
            return carry

        lax.fori_loop(0, N_SUB - 1, subs, 0)
        for o in organs[:-1]:
            visit(o, sub)

    barrier = pltpu.get_barrier_semaphore()
    each_peer(
        lambda o, s: pl.semaphore_signal(barrier, inc=1, device_id=(o, s), device_id_type=MESH)
    )

    loads = [pltpu.make_async_copy(mortar_hbm, m_stage, load_sem.at[0])]
    q_ref[...] = jnp.zeros(q_ref.shape, F32)
    qt_ref[...] = jnp.zeros(qt_ref.shape, F32)
    q_loads = [pltpu.make_async_copy(coarse_hbm, q_stage, load_sem.at[1])]
    x_loads = [pltpu.make_async_copy(warm_hbm, x_stage, load_sem.at[6])]
    r_loads = [pltpu.make_async_copy(rhs_hbm, r_stage, load_sem.at[11])]
    g_loads = [
        pltpu.make_async_copy(inv_hbm.at[f], g_stage.at[f], load_sem.at[16 + f])
        for f in range(faces)
    ]
    for copy in loads + q_loads + x_loads + r_loads + g_loads:
        copy.start()

    def start_round(i):
        n = ROWS[i]
        sb, rb = sends[i], recvs[i]

        def send(o, s):
            pltpu.make_async_remote_copy(
                sb.at[pl.ds((o * N_SUB + s) * n, n)],
                rb.at[pl.ds(me * n, n)],
                send_sem.at[i],
                recv_sem.at[i],
                device_id=(o, s),
                device_id_type=MESH,
            ).start()

        each_peer(send)
        pltpu.make_async_copy(
            sb.at[pl.ds(me * n, n)], rb.at[pl.ds(me * n, n)], self_sem.at[i]
        ).start()

    def wait_round(i):
        n = ROWS[i]
        sb, rb = sends[i], recvs[i]
        pltpu.make_async_copy(
            sb.at[pl.ds(me * n, n)], rb.at[pl.ds(me * n, n)], self_sem.at[i]
        ).wait()
        most = pl.ds(0, (N_DEV - 1) * n)
        pltpu.make_async_copy(rb.at[most], rb.at[most], recv_sem.at[i]).wait()
        pltpu.make_async_copy(sb.at[most], sb.at[most], send_sem.at[i]).wait()

    def put(i, j, value):
        sends[i][pl.ds(j, N_DEV, stride=ROWS[i]), :] = value

    def got(i, j):
        return recvs[i][pl.ds(j, N_DEV, stride=ROWS[i]), :]

    def partners():
        out = []
        for r in range(3):
            step = 2**r
            out.append((org, sub + step * (1 - 2 * ((sub // step) % 2))))
        for r in range(2):
            step = 2**r
            out.append((org + step * (1 - 2 * ((org // step) % 2)), sub))
        return out

    face_of = [rounds_ref[0, r] for r in range(N_MATCH)]
    round_of = []
    for f in range(faces):
        found = jnp.int32(0)
        for r in range(1, N_MATCH):
            found = jnp.where(face_of[r] == f, r, found)
        round_of.append(found)

    def start_match(source, send, recv, s_sem, r_sem):
        copies = []
        for r, dev in enumerate(partners()):
            send[r] = source[face_of[r]]
        for r, dev in enumerate(partners()):
            copy = pltpu.make_async_remote_copy(
                send.at[r], recv.at[r], s_sem.at[r], r_sem.at[r], device_id=dev, device_id_type=MESH
            )
            copy.start()
            copies.append(copy)
        return copies

    live = (active_ref[...] > 0) & (iota((1, rows), 1) < counts_ref[0, 0])
    owner = jnp.where(live, owner_ref[...], -1)
    owned = iota((N_DEV, rows), 0) == owner
    before = (iota((rows, rows), 0) < iota((rows, rows), 1)).astype(F32).astype(BF16)
    earlier = dot(owned.astype(F32).astype(BF16), before)
    rank = jnp.sum(jnp.where(owned, earlier, 0.0), axis=0, keepdims=True).astype(jnp.int32)
    slot = jnp.where(live, rank * N_DEV + owner, -1)
    dof_plus = dofs_ref[...].astype(F32) + 1.0
    lane = iota((N_DEV, LANES), 1)
    table = jnp.zeros((N_DEV, LANES), F32)
    for k in range(CAP):
        chosen = iota((N_DEV, rows), 0) + k * N_DEV == slot
        pick_ref[k] = chosen.astype(F32).astype(BF16)
        column = jnp.sum(jnp.where(chosen, dof_plus, 0.0), axis=1, keepdims=True) - 1.0
        table = jnp.where(lane == k, column, table)

    for copy in q_loads:
        copy.wait()
    for f in range(faces):
        q_ref[f, :modes] = q_stage[:, f, :]
    gram = jnp.zeros((8, LANES), F32)
    for f in range(faces):
        own = q_ref[f, :8]
        tiled = jnp.concatenate([own] * (LANES // 8), axis=0)
        gram = gram + lax.dot_general(
            own, tiled, (((1,), (1,)), ((), ())), precision=lax.Precision.HIGHEST,
            preferred_element_type=F32,
        )
    keep = iota((8, LANES), 1) // 8 == iota((8, LANES), 0) + 8
    table = table + jnp.sum(jnp.where(keep, gram, 0.0), axis=0, keepdims=True)
    put(0, 0, table)
    pl.semaphore_wait(barrier, N_DEV - 1)
    start_round(0)

    for copy in loads:
        copy.wait()
    m_high, m_low = split2(m_stage[...])

    def arrange(k, carry):
        at = pl.ds(pl.multiple_of(k * N_DEV, N_DEV), N_DEV)
        for part, back, ahead in ((m_high, wb_high, wf_high), (m_low, wb_low, wf_low)):
            block = dot(pick_ref[k], part)
            back[at, :] = block.astype(BF16)
            ahead[:, at] = block.T.astype(BF16)
        return carry

    lax.fori_loop(0, CAP, arrange, 0)

    eye = [iota((dirs, LANES), 1) == iota((dirs, LANES), 0) + dirs * m for m in range(8)]

    def to_row(columns):
        total = jnp.zeros((dirs, LANES), F32)
        for m, column in columns:
            total = total + jnp.where(eye[m], column, 0.0)
        return jnp.sum(total, axis=0, keepdims=True)

    def to_column(row, m):
        return jnp.sum(jnp.where(eye[m], row, 0.0), axis=1, keepdims=True)

    def inner(a_ref, b_ref):
        total = a_ref[0] * b_ref[0]
        for f in range(1, faces):
            total = total + a_ref[f] * b_ref[f]
        return jnp.sum(total, axis=1, keepdims=True)

    for copy in r_loads:
        copy.wait()
    for f in range(faces):
        r_ref[f] = r_stage[:, f, :]
    rhs_modes = []
    for m in range(modes):
        total = r_ref[0] * q_ref[0, m : m + 1]
        for f in range(1, faces):
            total = total + r_ref[f] * q_ref[f, m : m + 1]
        rhs_modes.append((m, jnp.sum(total, axis=1, keepdims=True)))
    rhs_row = to_row(rhs_modes)

    for copy in x_loads:
        copy.wait()
    for f in range(faces):
        p_ref[f] = x_stage[:, f, :]
    copies = start_match(p_ref, msend.at[0], mrecv[0], ms_sem.at[0], mr_sem.at[0])
    for r in range(N_MATCH):
        qsend[r] = q_ref[face_of[r], :8]
    q_copies = []
    for r, dev in enumerate(partners()):
        copy = pltpu.make_async_remote_copy(
            qsend.at[r], qrecv.at[r], qs_sem.at[r], qr_sem.at[r], device_id=dev, device_id_type=MESH
        )
        copy.start()
        q_copies.append(copy)

    wait_round(0)
    table = recvs[0][...]
    table_t = table.T
    in_group = iota((N_DEV, LANES), 0) // N_SUB == org
    gram_row = jnp.sum(jnp.where(in_group, table, 0.0), axis=0, keepdims=True)
    for k in range(CAP):
        column = table[:, k : k + 1].astype(jnp.int32)
        hit = iota((N_DEV, length), 1) == column
        wb_high[slots + k * N_DEV : slots + (k + 1) * N_DEV, :] = jnp.where(hit, -1.0, 0.0).astype(BF16)
        hit = iota((length, N_DEV), 0) == table_t[k : k + 1, :].astype(jnp.int32)
        wf_high[:, slots + k * N_DEV : slots + (k + 1) * N_DEV] = jnp.where(hit, 1.0, 0.0).astype(BF16)

    def row_values(x):
        n = x.shape[0]
        high, mid, low = split3(x)
        full = dot(jnp.concatenate([high, mid, low], axis=0), wf_high[...])
        fine = dot(jnp.concatenate([high, mid], axis=0), wf_low[...])
        full = full[:n] + (full[n : 2 * n] + full[2 * n :])
        return full[:, :slots] + (fine[:n] + fine[n:]), full[:, slots:]

    def spread_gaps(gaps):
        n = gaps.shape[0]
        high, mid, low = split3(gaps)
        full = dot(jnp.concatenate([high, mid, low], axis=0), wb_high[...])
        fine = dot(jnp.concatenate([high[:, :slots], mid[:, :slots]], axis=0), wb_low[...])
        return full[:n] + (full[n : 2 * n] + fine[:n] + (full[2 * n :] + fine[n:]))

    def stacked(value):
        return jnp.concatenate(
            [value[:, k * N_DEV : (k + 1) * N_DEV] for k in range(CAP)], axis=0
        )

    def unstacked(value):
        n = value.shape[0] // CAP
        return jnp.concatenate([value[k * n : (k + 1) * n] for k in range(CAP)], axis=1)

    def face_gaps(i, mine_a, mine_s):
        theirs_a, theirs_s = got(i, 0).T, got(i, 1).T
        return jnp.concatenate(
            [unstacked(mine_a - theirs_s), unstacked(theirs_a - mine_s)], axis=1
        )

    both_a, both_s = row_values(jnp.concatenate([p_ref[0], q_ref[0]], axis=0))
    mine_a, mine_s = stacked(both_a[:dirs]), stacked(both_s[:dirs])
    qa, qs = both_a[dirs : dirs + 8], both_s[dirs : dirs + 8]
    put(1, 0, mine_a.T)
    put(1, 1, mine_s.T)
    put(1, 2, jnp.broadcast_to(rhs_row, (N_DEV, LANES)))
    put(1, 3, jnp.concatenate([stacked(qa), stacked(qs)], axis=0).T)
    start_round(1)

    def gram_at(i, j):
        at = 64 + 8 * i + j
        return gram_row[:, at : at + 1]

    factor, inverse = {}, []
    for j in range(modes):
        pivot = gram_at(j, j)
        for k in range(j):
            pivot = pivot - factor[j, k] * factor[j, k]
        pivot = jnp.sqrt(pivot)
        inverse.append(1.0 / pivot)
        for i in range(j + 1, modes):
            value = gram_at(i, j)
            for k in range(j):
                value = value - factor[i, k] * factor[j, k]
            factor[i, j] = value * inverse[j]
    for f in range(faces):
        made = []
        for i in range(modes):
            row = q_ref[f, i : i + 1]
            for k in range(i):
                row = row - factor[i, k] * made[k]
            made.append(row * inverse[i])
            qt_ref[f, i : i + 1] = made[i]

    chunk = 64
    for f in range(faces):
        g_loads[f].wait()

        def halve(i, carry, f=f):
            at = pl.ds(pl.multiple_of(i * chunk, chunk), chunk)
            high, low = split2(g_stage[f, at, :])
            g_high[f, at, :] = high
            g_low[f, at, :] = low
            return carry

        lax.fori_loop(0, length // chunk, halve, 0)

    rho = None
    c_res = None
    for t in range(ITERS + 1):
        a_round = 1 + 2 * t
        for copy in copies:
            copy.wait()
        halo = mrecv[2 * t]
        for f in range(faces):
            yp_ref[f] = p_ref[f] - halo[round_of[f]]

        def smooth_face(f, carry):
            ym_ref[f] = mm(
                yp_ref[f], g_high[f], g_low[f]
            )
            return carry

        lax.fori_loop(1, faces, smooth_face, 0)

        wait_round(a_round)
        gaps = face_gaps(a_round, mine_a, mine_s)
        if t == 0:
            for copy in q_copies:
                copy.wait()
            c_row = jnp.sum(jnp.where(in_group, got(1, 2), 0.0), axis=0, keepdims=True)
            c_res = [to_column(c_row, m) for m in range(modes)]
            theirs = got(1, 3).T
            organ_row = iota((8, LANES), 0)
            of_peer = iota((8, LANES), 1) // N_SUB == organ_row
            mine = organ_row == org
            blocks = []
            for m in range(modes):
                outs, ins = [], []
                for k in range(CAP):
                    at = slice(k * N_DEV, (k + 1) * N_DEV)
                    ta = theirs[k * 8 + m : k * 8 + m + 1]
                    ts = theirs[64 + k * 8 + m : 64 + k * 8 + m + 1]
                    outs.append(
                        jnp.where(mine, qa[m : m + 1, at], 0.0) - jnp.where(of_peer, ts, 0.0)
                    )
                    ins.append(
                        jnp.where(of_peer, ta, 0.0) - jnp.where(mine, qs[m : m + 1, at], 0.0)
                    )
                blocks.append(jnp.concatenate(outs + ins, axis=1))
            mode_gaps = jnp.concatenate(blocks, axis=0)
            both = spread_gaps(jnp.concatenate([gaps, mode_gaps], axis=0))
            contact, mode_contact = both[:dirs], both[dirs:]
            organ_col = iota((8, length), 0)
            for f in range(faces):
                at_round = round_of[f]
                other = jnp.where(
                    at_round < 3,
                    org,
                    jnp.where(
                        at_round == 3, org + 1 - 2 * (org % 2), org + 2 - 4 * ((org // 2) % 2)
                    ),
                )
                arrived = qrecv[at_round]
                parts = []
                for m in range(modes):
                    part = jnp.where(organ_col == org, q_ref[f, m : m + 1], 0.0) - jnp.where(
                        organ_col == other, arrived[m : m + 1], 0.0
                    )
                    if f == 0:
                        part = part + mode_contact[8 * m : 8 * m + 8]
                    parts.append(part)
                parts.append(jnp.zeros((LANES - 8 * modes, length), F32))
                wide = jnp.concatenate(parts, axis=0).T
                high, low = split2(wide)
                wt_high[f] = high
                wt_low[f] = low
        else:
            contact = spread_gaps(gaps)
            rho_new = to_column(jnp.sum(got(a_round, 2), axis=0, keepdims=True), 0)
            beta = rho_new / rho if t > 1 else None
            rho = rho_new
        yp_ref[0] = yp_ref[0] + contact
        ym_ref[0] = mm(yp_ref[0], g_high[0], g_low[0])

        for f in range(faces):
            made = ym_ref[f]
            if t > 1:
                w_ref[f] = yp_ref[f] + beta * w_ref[f]
                y_ref[f] = made + beta * y_ref[f]
                d_ref[f] = p_ref[f] + beta * d_ref[f]
            else:
                w_ref[f] = yp_ref[f]
                y_ref[f] = made
                d_ref[f] = p_ref[f]
        curved = inner(w_ref, y_ref)

        b_round = a_round + 1
        if t == ITERS:
            put(b_round, 0, jnp.broadcast_to(to_row([(0, curved)]), (N_DEV, LANES)))
            start_round(b_round)
            wait_round(b_round)
            step = rho / to_column(jnp.sum(recvs[b_round][...], axis=0, keepdims=True), 0)
            for f in range(faces):
                sol_ref[f] = sol_ref[f] + step * d_ref[f]
            break

        copies = start_match(
            y_ref, msend.at[2 * t + 1], mrecv[2 * t + 1], ms_sem.at[2 * t + 1], mr_sem.at[2 * t + 1]
        )
        mine_a, mine_s = row_values(y_ref[0])
        mine_a, mine_s = stacked(mine_a), stacked(mine_s)
        put(b_round, 0, mine_a.T)
        put(b_round, 1, mine_s.T)
        coarse = mm(y_ref[0], wt_high[0], wt_low[0])
        for f in range(1, faces):
            coarse = coarse + mm(y_ref[f], wt_high[f], wt_low[f])
        coarse = jnp.concatenate([coarse, jnp.zeros((LANES - dirs, LANES), F32)], axis=0).T
        parts = [coarse[8 * m : 8 * m + 8, :dirs] for m in range(modes)]
        parts.append(jnp.zeros((8, LANES - modes * dirs), F32))
        coarse = jnp.concatenate(parts, axis=1) + to_row([(modes, curved)])
        for o in range(N_ORG):
            sends[b_round][pl.ds(o * N_SUB * ROWS[b_round] + 2, N_SUB, stride=ROWS[b_round]), :] = (
                jnp.broadcast_to(coarse[o : o + 1], (N_SUB, LANES))
            )
        start_round(b_round)

        for copy in copies:
            copy.wait()
        halo = mrecv[2 * t + 1]
        for f in range(faces):
            yp_ref[f] = y_ref[f] - halo[round_of[f]]
        wait_round(b_round)
        yp_ref[0] = yp_ref[0] + spread_gaps(face_gaps(b_round, mine_a, mine_s))
        total = jnp.sum(got(b_round, 2), axis=0, keepdims=True)
        c_image = [to_column(total, m) for m in range(modes)]
        if t > 0:
            step = rho / to_column(total, modes)
        for f in range(faces):
            if t > 0:
                sol_ref[f] = sol_ref[f] + step * d_ref[f]
                r_ref[f] = r_ref[f] - step * yp_ref[f]
            else:
                sol_ref[f] = d_ref[f]
                r_ref[f] = r_ref[f] - yp_ref[f]
        for m in range(modes):
            c_res[m] = c_res[m] - (step * c_image[m] if t > 0 else c_image[m])
        solved = []
        for i in range(modes):
            value = c_res[i]
            for k in range(i):
                value = value - factor[i, k] * solved[k]
            solved.append(value * inverse[i])
        for f in range(faces):
            value = r_ref[f]
            for m in range(modes):
                value = value - solved[m] * qt_ref[f, m : m + 1]
            p_ref[f] = value

        n_halo = 2 * t + 2
        copies = start_match(
            p_ref, msend.at[n_halo], mrecv[n_halo], ms_sem.at[n_halo], mr_sem.at[n_halo]
        )
        mine_a, mine_s = row_values(p_ref[0])
        mine_a, mine_s = stacked(mine_a), stacked(mine_s)
        put(b_round + 1, 0, mine_a.T)
        put(b_round + 1, 1, mine_s.T)
        put(
            b_round + 1,
            2,
            jnp.broadcast_to(to_row([(0, inner(r_ref, p_ref))]), (N_DEV, LANES)),
        )
        start_round(b_round + 1)

    for f in range(faces):
        x_stage[:, f, :] = sol_ref[f]
    write = pltpu.make_async_copy(x_stage, out_hbm, out_sem.at[0])
    write.start()
    write.wait()


def local(
    dual_rhs,
    warm_start,
    inverse_blocks,
    coarse_basis,
    mortar_rows,
    match_rounds,
    slave_owner,
    slave_dofs,
    active_set,
    row_counts,
):
    dirs, _, _, faces, length = dual_rhs.shape
    rows = mortar_rows.shape[2]
    modes = coarse_basis.shape[0]
    slots = CAP * N_DEV
    field = pltpu.VMEM((faces, dirs, length), F32)
    dma = pltpu.SemaphoreType.DMA
    any_spec = pl.BlockSpec(memory_space=pl.ANY)
    vmem_spec = pl.BlockSpec(memory_space=pltpu.VMEM)
    smem_spec = pl.BlockSpec(memory_space=pltpu.SMEM)
    scratch = [
        pltpu.VMEM((faces, length, length), F32),
        pltpu.VMEM((faces, length, length), BF16),
        pltpu.VMEM((faces, length, length), BF16),
        pltpu.VMEM((rows, length), F32),
        pltpu.VMEM((CAP, N_DEV, rows), BF16),
        pltpu.VMEM((length, 2 * slots), BF16),
        pltpu.VMEM((length, slots), BF16),
        pltpu.VMEM((2 * slots, length), BF16),
        pltpu.VMEM((slots, length), BF16),
        pltpu.VMEM((faces, length, LANES), BF16),
        pltpu.VMEM((faces, length, LANES), BF16),
        field,
        pltpu.VMEM((faces, 8, length), F32),
    ]
    scratch += [field] * 8
    scratch += [
        pltpu.VMEM((modes, faces, length), F32),
        pltpu.VMEM((dirs, faces, length), F32),
        pltpu.VMEM((dirs, faces, length), F32),
        pltpu.VMEM((N_HALO, N_MATCH, dirs, length), F32),
        pltpu.VMEM((N_MATCH, 8, length), F32),
        pltpu.VMEM((N_MATCH, 8, length), F32),
    ]
    scratch += [pltpu.VMEM((N_DEV * n, LANES), F32) for n in ROWS] * 2
    scratch += [pltpu.VMEM((N_MATCH, dirs, length), F32)] * N_HALO
    scratch += [
        dma((21,)),
        dma((faces,)),
        dma((N_ROUND,)),
        dma((N_ROUND,)),
        dma((N_ROUND,)),
        dma((N_HALO, N_MATCH)),
        dma((N_HALO, N_MATCH)),
        dma((N_MATCH,)),
        dma((N_MATCH,)),
    ]
    result = pl.pallas_call(
        kernel,
        out_shape=jax.ShapeDtypeStruct((dirs, faces, length), F32),
        in_specs=[any_spec] * 5 + [vmem_spec] * 3 + [smem_spec] * 2,
        out_specs=any_spec,
        scratch_shapes=scratch,
        compiler_params=pltpu.CompilerParams(
            collective_id=0, has_side_effects=True, vmem_limit_bytes=60 * 2**20
        ),
    )(
        dual_rhs.reshape(dirs, faces, length),
        warm_start.reshape(dirs, faces, length),
        inverse_blocks.reshape(faces, length, length),
        coarse_basis.reshape(modes, faces, length),
        mortar_rows.reshape(rows, length),
        slave_owner.reshape(1, rows),
        slave_dofs.reshape(1, rows),
        active_set.reshape(1, rows),
        match_rounds.reshape(1, N_MATCH),
        row_counts.reshape(1, 1),
    )
    return result.reshape(dirs, 1, 1, faces, length)


def solution(mesh):
    in_specs = (
        P(None, "organ", "sub", None, None),
        P(None, "organ", "sub", None, None),
        P("organ", "sub", None, None, None),
        P(None, "organ", "sub", None, None),
        P("organ", "sub", None, None),
        P("organ", "sub", None),
        P("organ", "sub", None, None),
        P("organ", "sub", None),
        P("organ", "sub", None),
        P("organ", "sub", None),
    )
    out_specs = P(None, "organ", "sub", None, None)
    return jax.shard_map(local, mesh=mesh, in_specs=in_specs, out_specs=out_specs, check_vma=False)
```

```python
import jax
import jax.numpy as jnp
from jax import lax
from jax.experimental import pallas as pl
from jax.experimental.pallas import tpu as pltpu
from jax.sharding import PartitionSpec as P

ITERS = 3
CAP = 8
MESH = pl.DeviceIdType.MESH
F32 = jnp.float32
BF16 = jnp.bfloat16
N_ORG, N_SUB = 8, 16
N_DEV = N_ORG * N_SUB
LANES = 128
ROWS = (1, 4, 3, 3, 3, 3, 3, 3, 1)
N_ROUND = len(ROWS)
N_MATCH = 5
N_HALO = 2 * ITERS + 1


def iota(shape, dim):
    return lax.broadcasted_iota(jnp.int32, shape, dim)


def split2(x):
    high = x.astype(BF16)
    return high, (x - high.astype(F32)).astype(BF16)


def dot(a, b):
    return jnp.dot(a, b, preferred_element_type=F32)


def mm(x, w_high, w_low):
    n = x.shape[0]
    high, low = split2(x)
    a = dot(jnp.concatenate([high, low], axis=0), w_high)
    return a[:n] + (a[n:] + dot(high, w_low))


def offset_of(u):
    return u - (u // 2) * (2 * u - 5)


def kernel(
    rhs_hbm,
    warm_hbm,
    inv_hbm,
    coarse_hbm,
    mortar_hbm,
    owner_ref,
    dofs_ref,
    active_ref,
    rounds_ref,
    counts_ref,
    out_hbm,
    g_stage,
    g_high,
    g_low,
    m_stage,
    pick_ref,
    wf_high,
    wf_low,
    wb_high,
    wb_low,
    wt_high,
    wt_low,
    q_ref,
    qt_ref,
    p_ref,
    d_ref,
    w_ref,
    y_ref,
    yp_ref,
    ym_ref,
    r_ref,
    sol_ref,
    msend,
    qsend,
    qrecv,
    *rest,
):
    sends, recvs = rest[:N_ROUND], rest[N_ROUND : 2 * N_ROUND]
    mrecv = rest[2 * N_ROUND : 2 * N_ROUND + N_HALO]
    (load_sem, out_sem, send_sem, recv_sem, self_sem, ms_sem, mr_sem, qs_sem, qr_sem) = rest[
        2 * N_ROUND + N_HALO :
    ]
    faces, dirs, length = p_ref.shape
    rows = m_stage.shape[0]
    modes = coarse_hbm.shape[0]
    slots = CAP * N_DEV
    org, sub = lax.axis_index("organ"), lax.axis_index("sub")
    me = org * N_SUB + sub
    x_at, core_at, z_at, y_at = org // 2, org % 2, sub // 4, sub % 4

    organs = [
        ((x_at + dx) % 4) * 2 + (core_at + dc) % 2 for dx in (2, 3, 1, 0) for dc in (1, 0)
    ]

    def each_peer(visit):
        def subs(i, carry):
            z_to = (z_at + offset_of(3 - i // 4)) % 4
            y_to = (y_at + offset_of(3 - i % 4)) % 4
            for o in organs:
                visit(o, z_to * 4 + y_to)
            return carry

        lax.fori_loop(0, N_SUB - 1, subs, 0)
        for o in organs[:-1]:
            visit(o, sub)

    barrier = pltpu.get_barrier_semaphore()
    each_peer(
        lambda o, s: pl.semaphore_signal(barrier, inc=1, device_id=(o, s), device_id_type=MESH)
    )

    loads = [pltpu.make_async_copy(mortar_hbm, m_stage, load_sem.at[0])]
    q_ref[...] = jnp.zeros(q_ref.shape, F32)
    qt_ref[...] = jnp.zeros(qt_ref.shape, F32)
    q_loads = [
        pltpu.make_async_copy(
            coarse_hbm.at[:, f, 0], q_ref.at[f, pl.ds(0, modes)], load_sem.at[1 + f]
        )
        for f in range(faces)
    ]
    x_loads = [
        pltpu.make_async_copy(warm_hbm.at[:, f, 0], p_ref.at[f], load_sem.at[6 + f])
        for f in range(faces)
    ]
    r_loads = [
        pltpu.make_async_copy(rhs_hbm.at[:, f, 0], r_ref.at[f], load_sem.at[11 + f])
        for f in range(faces)
    ]
    g_loads = [
        pltpu.make_async_copy(inv_hbm.at[f], g_stage.at[f], load_sem.at[16 + f])
        for f in range(faces)
    ]
    for copy in loads + q_loads + x_loads + r_loads + g_loads:
        copy.start()

    def start_round(i):
        n = ROWS[i]
        sb, rb = sends[i], recvs[i]

        def send(o, s):
            pltpu.make_async_remote_copy(
                sb.at[pl.ds((o * N_SUB + s) * n, n)],
                rb.at[pl.ds(me * n, n)],
                send_sem.at[i],
                recv_sem.at[i],
                device_id=(o, s),
                device_id_type=MESH,
            ).start()

        each_peer(send)
        pltpu.make_async_copy(
            sb.at[pl.ds(me * n, n)], rb.at[pl.ds(me * n, n)], self_sem.at[i]
        ).start()

    def wait_round(i):
        n = ROWS[i]
        sb, rb = sends[i], recvs[i]
        pltpu.make_async_copy(
            sb.at[pl.ds(me * n, n)], rb.at[pl.ds(me * n, n)], self_sem.at[i]
        ).wait()
        most = pl.ds(0, (N_DEV - 1) * n)
        pltpu.make_async_copy(rb.at[most], rb.at[most], recv_sem.at[i]).wait()
        pltpu.make_async_copy(sb.at[most], sb.at[most], send_sem.at[i]).wait()

    def put(i, j, value):
        sends[i][pl.ds(j, N_DEV, stride=ROWS[i]), :] = value

    def got(i, j):
        return recvs[i][pl.ds(j, N_DEV, stride=ROWS[i]), :]

    def partners():
        out = []
        for r in range(3):
            step = 2**r
            out.append((org, sub + step * (1 - 2 * ((sub // step) % 2))))
        for r in range(2):
            step = 2**r
            out.append((org + step * (1 - 2 * ((org // step) % 2)), sub))
        return out

    face_of = [rounds_ref[0, r] for r in range(N_MATCH)]
    round_of = []
    for f in range(faces):
        found = jnp.int32(0)
        for r in range(1, N_MATCH):
            found = jnp.where(face_of[r] == f, r, found)
        round_of.append(found)

    def start_match(source, send, recv, s_sem, r_sem):
        copies = []
        for r, dev in enumerate(partners()):
            send[r] = source[face_of[r]]
        for r, dev in enumerate(partners()):
            copy = pltpu.make_async_remote_copy(
                send.at[r], recv.at[r], s_sem.at[r], r_sem.at[r], device_id=dev, device_id_type=MESH
            )
            copy.start()
            copies.append(copy)
        return copies

    live = (active_ref[...] > 0) & (iota((1, rows), 1) < counts_ref[0, 0])
    owner = jnp.where(live, owner_ref[...], -1)
    owned = iota((N_DEV, rows), 0) == owner
    before = (iota((rows, rows), 0) < iota((rows, rows), 1)).astype(F32).astype(BF16)
    earlier = dot(owned.astype(F32).astype(BF16), before)
    rank = jnp.sum(jnp.where(owned, earlier, 0.0), axis=0, keepdims=True).astype(jnp.int32)
    slot = jnp.where(live, rank * N_DEV + owner, -1)
    dof_plus = dofs_ref[...].astype(F32) + 1.0
    lane = iota((N_DEV, LANES), 1)
    table = jnp.zeros((N_DEV, LANES), F32)
    for k in range(CAP):
        chosen = iota((N_DEV, rows), 0) + k * N_DEV == slot
        pick_ref[k] = chosen.astype(F32).astype(BF16)
        column = jnp.sum(jnp.where(chosen, dof_plus, 0.0), axis=1, keepdims=True) - 1.0
        table = jnp.where(lane == k, column, table)

    for copy in q_loads:
        copy.wait()
    gram = jnp.zeros((8, LANES), F32)
    for f in range(faces):
        own = q_ref[f, :8]
        tiled = jnp.concatenate([own] * (LANES // 8), axis=0)
        gram = gram + lax.dot_general(
            own, tiled, (((1,), (1,)), ((), ())), precision=lax.Precision.HIGHEST,
            preferred_element_type=F32,
        )
    keep = iota((8, LANES), 1) // 8 == iota((8, LANES), 0) + 8
    table = table + jnp.sum(jnp.where(keep, gram, 0.0), axis=0, keepdims=True)
    put(0, 0, table)
    pl.semaphore_wait(barrier, N_DEV - 1)
    start_round(0)

    for copy in loads:
        copy.wait()
    m_high, m_low = split2(m_stage[...])

    def arrange(k, carry):
        at = pl.ds(pl.multiple_of(k * N_DEV, N_DEV), N_DEV)
        for part, back, ahead in ((m_high, wb_high, wf_high), (m_low, wb_low, wf_low)):
            block = dot(pick_ref[k], part)
            back[at, :] = block.astype(BF16)
            ahead[:, at] = block.T.astype(BF16)
        return carry

    lax.fori_loop(0, CAP, arrange, 0)

    eye = [iota((dirs, LANES), 1) == iota((dirs, LANES), 0) + dirs * m for m in range(8)]

    def to_row(columns):
        total = jnp.zeros((dirs, LANES), F32)
        for m, column in columns:
            total = total + jnp.where(eye[m], column, 0.0)
        return jnp.sum(total, axis=0, keepdims=True)

    def to_column(row, m):
        return jnp.sum(jnp.where(eye[m], row, 0.0), axis=1, keepdims=True)

    def inner(a_ref, b_ref):
        total = a_ref[0] * b_ref[0]
        for f in range(1, faces):
            total = total + a_ref[f] * b_ref[f]
        return jnp.sum(total, axis=1, keepdims=True)

    for copy in r_loads:
        copy.wait()
    rhs_modes = []
    for m in range(modes):
        total = r_ref[0] * q_ref[0, m : m + 1]
        for f in range(1, faces):
            total = total + r_ref[f] * q_ref[f, m : m + 1]
        rhs_modes.append((m, jnp.sum(total, axis=1, keepdims=True)))
    rhs_row = to_row(rhs_modes)

    for copy in x_loads:
        copy.wait()
    copies = start_match(p_ref, msend.at[0], mrecv[0], ms_sem.at[0], mr_sem.at[0])
    for r in range(N_MATCH):
        qsend[r] = q_ref[face_of[r], :8]
    q_copies = []
    for r, dev in enumerate(partners()):
        copy = pltpu.make_async_remote_copy(
            qsend.at[r], qrecv.at[r], qs_sem.at[r], qr_sem.at[r], device_id=dev, device_id_type=MESH
        )
        copy.start()
        q_copies.append(copy)

    wait_round(0)
    table = recvs[0][...]
    table_t = table.T
    in_group = iota((N_DEV, LANES), 0) // N_SUB == org
    gram_row = jnp.sum(jnp.where(in_group, table, 0.0), axis=0, keepdims=True)
    for k in range(CAP):
        hit = iota((length, N_DEV), 0) == table_t[k : k + 1, :].astype(jnp.int32)
        wf_high[:, slots + k * N_DEV : slots + (k + 1) * N_DEV] = jnp.where(hit, 1.0, 0.0).astype(BF16)

    def row_values(x):
        n = x.shape[0]
        high, low = split2(x)
        full = dot(jnp.concatenate([high, low], axis=0), wf_high[...])
        full = full[:n] + full[n:]
        return full[:, :slots] + dot(high, wf_low[...]), full[:, slots:]

    def spread_gaps(gaps):
        n = gaps.shape[0]
        high, low = split2(gaps)
        full = dot(jnp.concatenate([high, low], axis=0), wb_high[...])
        return full[:n] + (full[n:] + dot(high[:, :slots], wb_low[...]))

    def stacked(value):
        return jnp.concatenate(
            [value[:, k * N_DEV : (k + 1) * N_DEV] for k in range(CAP)], axis=0
        )

    def unstacked(value):
        n = value.shape[0] // CAP
        return jnp.concatenate([value[k * n : (k + 1) * n] for k in range(CAP)], axis=1)

    def face_gaps(i, mine_a, mine_s):
        theirs_a, theirs_s = got(i, 0).T, got(i, 1).T
        return jnp.concatenate(
            [unstacked(mine_a - theirs_s), unstacked(theirs_a - mine_s)], axis=1
        )

    both_a, both_s = row_values(jnp.concatenate([p_ref[0], q_ref[0]], axis=0))
    mine_a, mine_s = stacked(both_a[:dirs]), stacked(both_s[:dirs])
    qa, qs = both_a[dirs : dirs + 8], both_s[dirs : dirs + 8]
    put(1, 0, mine_a.T)
    put(1, 1, mine_s.T)
    put(1, 2, jnp.broadcast_to(rhs_row, (N_DEV, LANES)))
    put(1, 3, jnp.concatenate([stacked(qa), stacked(qs)], axis=0).T)
    start_round(1)

    for k in range(CAP):
        column = table[:, k : k + 1].astype(jnp.int32)
        hit = iota((N_DEV, length), 1) == column
        wb_high[slots + k * N_DEV : slots + (k + 1) * N_DEV, :] = jnp.where(hit, -1.0, 0.0).astype(BF16)

    def gram_at(i, j):
        at = 64 + 8 * i + j
        return gram_row[:, at : at + 1]

    factor, inverse = {}, []
    for j in range(modes):
        pivot = gram_at(j, j)
        for k in range(j):
            pivot = pivot - factor[j, k] * factor[j, k]
        pivot = jnp.sqrt(pivot)
        inverse.append(1.0 / pivot)
        for i in range(j + 1, modes):
            value = gram_at(i, j)
            for k in range(j):
                value = value - factor[i, k] * factor[j, k]
            factor[i, j] = value * inverse[j]
    for f in range(faces):
        made = []
        for i in range(modes):
            row = q_ref[f, i : i + 1]
            for k in range(i):
                row = row - factor[i, k] * made[k]
            made.append(row * inverse[i])
            qt_ref[f, i : i + 1] = made[i]

    chunk = 64
    for f in range(faces):
        g_loads[f].wait()

        def halve(i, carry, f=f):
            at = pl.ds(pl.multiple_of(i * chunk, chunk), chunk)
            high, low = split2(g_stage[f, at, :])
            g_high[f, at, :] = high
            g_low[f, at, :] = low
            return carry

        lax.fori_loop(0, length // chunk, halve, 0)

    def make_wide(f, extra):
        at_round = round_of[f]
        other = jnp.where(
            at_round < 3,
            org,
            jnp.where(at_round == 3, org + 1 - 2 * (org % 2), org + 2 - 4 * ((org // 2) % 2)),
        )
        arrived = qrecv[at_round]
        organ_col = iota((8, length), 0)
        parts = []
        for m in range(modes):
            part = jnp.where(organ_col == org, q_ref[f, m : m + 1], 0.0) - jnp.where(
                organ_col == other, arrived[m : m + 1], 0.0
            )
            if extra is not None:
                part = part + extra[8 * m : 8 * m + 8]
            parts.append(part)
        parts.append(jnp.zeros((LANES - 8 * modes, length), F32))
        high, low = split2(jnp.concatenate(parts, axis=0).T)
        wt_high[f] = high
        wt_low[f] = low

    rho = None
    c_res = None
    coarse_rest = None
    for t in range(ITERS + 1):
        a_round = 1 + 2 * t
        for copy in copies:
            copy.wait()
        halo = mrecv[2 * t]
        for f in range(faces):
            yp_ref[f] = p_ref[f] - halo[round_of[f]]

        def smooth_face(f, carry):
            ym_ref[f] = mm(
                yp_ref[f], g_high[f], g_low[f]
            )
            return carry

        lax.fori_loop(1, faces, smooth_face, 0)
        if t == 0:
            for copy in q_copies:
                copy.wait()
            for f in range(1, faces):
                make_wide(f, None)
        if t < ITERS:
            coarse_part = mm(ym_ref[1], wt_high[1], wt_low[1])
            for f in range(2, faces):
                coarse_part = coarse_part + mm(ym_ref[f], wt_high[f], wt_low[f])

        wait_round(a_round)
        gaps = face_gaps(a_round, mine_a, mine_s)
        if t == 0:
            c_row = jnp.sum(jnp.where(in_group, got(1, 2), 0.0), axis=0, keepdims=True)
            c_res = [to_column(c_row, m) for m in range(modes)]
            theirs = got(1, 3).T
            organ_row = iota((8, LANES), 0)
            of_peer = iota((8, LANES), 1) // N_SUB == organ_row
            mine = organ_row == org
            blocks = []
            for m in range(modes):
                outs, ins = [], []
                for k in range(CAP):
                    at = slice(k * N_DEV, (k + 1) * N_DEV)
                    ta = theirs[k * 8 + m : k * 8 + m + 1]
                    ts = theirs[64 + k * 8 + m : 64 + k * 8 + m + 1]
                    outs.append(
                        jnp.where(mine, qa[m : m + 1, at], 0.0) - jnp.where(of_peer, ts, 0.0)
                    )
                    ins.append(
                        jnp.where(of_peer, ta, 0.0) - jnp.where(mine, qs[m : m + 1, at], 0.0)
                    )
                blocks.append(jnp.concatenate(outs + ins, axis=1))
            mode_gaps = jnp.concatenate(blocks, axis=0)
            both = spread_gaps(jnp.concatenate([gaps, mode_gaps], axis=0))
            contact, mode_contact = both[:dirs], both[dirs:]
            make_wide(0, mode_contact)
        else:
            contact = spread_gaps(gaps)
            rho_new = to_column(jnp.sum(got(a_round, 2), axis=0, keepdims=True), 0)
            beta = rho_new / rho if t > 1 else None
            rho = rho_new
        yp_ref[0] = yp_ref[0] + contact
        ym_ref[0] = mm(yp_ref[0], g_high[0], g_low[0])

        for f in range(faces):
            made = ym_ref[f]
            if t > 1:
                w_ref[f] = yp_ref[f] + beta * w_ref[f]
                y_ref[f] = made + beta * y_ref[f]
                d_ref[f] = p_ref[f] + beta * d_ref[f]
            else:
                w_ref[f] = yp_ref[f]
                y_ref[f] = made
                d_ref[f] = p_ref[f]
        curved = inner(w_ref, y_ref)

        b_round = a_round + 1
        if t == ITERS:
            put(b_round, 0, jnp.broadcast_to(to_row([(0, curved)]), (N_DEV, LANES)))
            start_round(b_round)
            wait_round(b_round)
            step = rho / to_column(jnp.sum(recvs[b_round][...], axis=0, keepdims=True), 0)
            for f in range(faces):
                sol_ref[f] = sol_ref[f] + step * d_ref[f]
            break

        copies = start_match(
            y_ref, msend.at[2 * t + 1], mrecv[2 * t + 1], ms_sem.at[2 * t + 1], mr_sem.at[2 * t + 1]
        )
        mine_a, mine_s = row_values(y_ref[0])
        mine_a, mine_s = stacked(mine_a), stacked(mine_s)
        put(b_round, 0, mine_a.T)
        put(b_round, 1, mine_s.T)
        coarse_rest = coarse_part + beta * coarse_rest if t > 1 else coarse_part
        coarse = coarse_rest + mm(y_ref[0], wt_high[0], wt_low[0])
        coarse = jnp.concatenate([coarse, jnp.zeros((LANES - dirs, LANES), F32)], axis=0).T
        parts = [coarse[8 * m : 8 * m + 8, :dirs] for m in range(modes)]
        parts.append(jnp.zeros((8, LANES - modes * dirs), F32))
        coarse = jnp.concatenate(parts, axis=1) + to_row([(modes, curved)])
        for o in range(N_ORG):
            sends[b_round][pl.ds(o * N_SUB * ROWS[b_round] + 2, N_SUB, stride=ROWS[b_round]), :] = (
                jnp.broadcast_to(coarse[o : o + 1], (N_SUB, LANES))
            )
        start_round(b_round)

        for copy in copies:
            copy.wait()
        halo = mrecv[2 * t + 1]
        for f in range(faces):
            yp_ref[f] = y_ref[f] - halo[round_of[f]]
        wait_round(b_round)
        yp_ref[0] = yp_ref[0] + spread_gaps(face_gaps(b_round, mine_a, mine_s))
        total = jnp.sum(got(b_round, 2), axis=0, keepdims=True)
        c_image = [to_column(total, m) for m in range(modes)]
        if t > 0:
            step = rho / to_column(total, modes)
        for f in range(faces):
            if t > 0:
                sol_ref[f] = sol_ref[f] + step * d_ref[f]
                r_ref[f] = r_ref[f] - step * yp_ref[f]
            else:
                sol_ref[f] = d_ref[f]
                r_ref[f] = r_ref[f] - yp_ref[f]
        for m in range(modes):
            c_res[m] = c_res[m] - (step * c_image[m] if t > 0 else c_image[m])
        solved = []
        for i in range(modes):
            value = c_res[i]
            for k in range(i):
                value = value - factor[i, k] * solved[k]
            solved.append(value * inverse[i])
        for f in range(faces):
            value = r_ref[f]
            for m in range(modes):
                value = value - solved[m] * qt_ref[f, m : m + 1]
            p_ref[f] = value

        n_halo = 2 * t + 2
        copies = start_match(
            p_ref, msend.at[n_halo], mrecv[n_halo], ms_sem.at[n_halo], mr_sem.at[n_halo]
        )
        mine_a, mine_s = row_values(p_ref[0])
        mine_a, mine_s = stacked(mine_a), stacked(mine_s)
        put(b_round + 1, 0, mine_a.T)
        put(b_round + 1, 1, mine_s.T)
        put(
            b_round + 1,
            2,
            jnp.broadcast_to(to_row([(0, inner(r_ref, p_ref))]), (N_DEV, LANES)),
        )
        start_round(b_round + 1)

    writes = [
        pltpu.make_async_copy(sol_ref.at[f], out_hbm.at[:, f, 0], out_sem.at[f])
        for f in range(faces)
    ]
    for copy in writes:
        copy.start()
    for copy in writes:
        copy.wait()


def local(
    dual_rhs,
    warm_start,
    inverse_blocks,
    coarse_basis,
    mortar_rows,
    match_rounds,
    slave_owner,
    slave_dofs,
    active_set,
    row_counts,
):
    dirs, _, _, faces, length = dual_rhs.shape
    rows = mortar_rows.shape[2]
    modes = coarse_basis.shape[0]
    slots = CAP * N_DEV
    field = pltpu.VMEM((faces, dirs, length), F32)
    dma = pltpu.SemaphoreType.DMA
    any_spec = pl.BlockSpec(memory_space=pl.ANY)
    vmem_spec = pl.BlockSpec(memory_space=pltpu.VMEM)
    smem_spec = pl.BlockSpec(memory_space=pltpu.SMEM)
    scratch = [
        pltpu.VMEM((faces, length, length), F32),
        pltpu.VMEM((faces, length, length), BF16),
        pltpu.VMEM((faces, length, length), BF16),
        pltpu.VMEM((rows, length), F32),
        pltpu.VMEM((CAP, N_DEV, rows), BF16),
        pltpu.VMEM((length, 2 * slots), BF16),
        pltpu.VMEM((length, slots), BF16),
        pltpu.VMEM((2 * slots, length), BF16),
        pltpu.VMEM((slots, length), BF16),
        pltpu.VMEM((faces, length, LANES), BF16),
        pltpu.VMEM((faces, length, LANES), BF16),
        field,
        pltpu.VMEM((faces, 8, length), F32),
    ]
    scratch += [field] * 8
    scratch += [
        pltpu.VMEM((N_HALO, N_MATCH, dirs, length), F32),
        pltpu.VMEM((N_MATCH, 8, length), F32),
        pltpu.VMEM((N_MATCH, 8, length), F32),
    ]
    scratch += [pltpu.VMEM((N_DEV * n, LANES), F32) for n in ROWS] * 2
    scratch += [pltpu.VMEM((N_MATCH, dirs, length), F32)] * N_HALO
    scratch += [
        dma((21,)),
        dma((faces,)),
        dma((N_ROUND,)),
        dma((N_ROUND,)),
        dma((N_ROUND,)),
        dma((N_HALO, N_MATCH)),
        dma((N_HALO, N_MATCH)),
        dma((N_MATCH,)),
        dma((N_MATCH,)),
    ]
    result = pl.pallas_call(
        kernel,
        out_shape=jax.ShapeDtypeStruct((dirs, faces, 1, length), F32),
        in_specs=[any_spec] * 5 + [vmem_spec] * 3 + [smem_spec] * 2,
        out_specs=any_spec,
        scratch_shapes=scratch,
        compiler_params=pltpu.CompilerParams(
            collective_id=0, has_side_effects=True, vmem_limit_bytes=60 * 2**20
        ),
    )(
        dual_rhs.reshape(dirs, faces, 1, length),
        warm_start.reshape(dirs, faces, 1, length),
        inverse_blocks.reshape(faces, length, length),
        coarse_basis.reshape(modes, faces, 1, length),
        mortar_rows.reshape(rows, length),
        slave_owner.reshape(1, rows),
        slave_dofs.reshape(1, rows),
        active_set.reshape(1, rows),
        match_rounds.reshape(1, N_MATCH),
        row_counts.reshape(1, 1),
    )
    return result.reshape(dirs, 1, 1, faces, length)


def solution(mesh):
    in_specs = (
        P(None, "organ", "sub", None, None),
        P(None, "organ", "sub", None, None),
        P("organ", "sub", None, None, None),
        P(None, "organ", "sub", None, None),
        P("organ", "sub", None, None),
        P("organ", "sub", None),
        P("organ", "sub", None, None),
        P("organ", "sub", None),
        P("organ", "sub", None),
        P("organ", "sub", None),
    )
    out_specs = P(None, "organ", "sub", None, None)
    return jax.shard_map(local, mesh=mesh, in_specs=in_specs, out_specs=out_specs, check_vma=False)
```

```python
import jax
import jax.numpy as jnp
from jax import lax
from jax.experimental import pallas as pl
from jax.experimental.pallas import tpu as pltpu
from jax.sharding import PartitionSpec as P

ITERS = 3
CAP = 8
MESH = pl.DeviceIdType.MESH
F32 = jnp.float32
BF16 = jnp.bfloat16
N_ORG, N_SUB = 8, 16
N_DEV = N_ORG * N_SUB
LANES = 128
ROWS = (1, 4, 3, 3, 3, 3, 3, 3, 1)
N_ROUND = len(ROWS)
N_MATCH = 5
N_HALO = 2 * ITERS + 1


def iota(shape, dim):
    return lax.broadcasted_iota(jnp.int32, shape, dim)


def split2(x):
    high = x.astype(BF16)
    return high, (x - high.astype(F32)).astype(BF16)


def dot(a, b):
    return jnp.dot(a, b, preferred_element_type=F32)


def mm(x, w_high, w_low):
    n = x.shape[0]
    high, low = split2(x)
    a = dot(jnp.concatenate([high, low], axis=0), w_high)
    return a[:n] + (a[n:] + dot(high, w_low))


def offset_of(u):
    return u - (u // 2) * (2 * u - 5)


def kernel(
    rhs_hbm,
    warm_hbm,
    inv_hbm,
    coarse_hbm,
    mortar_hbm,
    owner_ref,
    dofs_ref,
    active_ref,
    rounds_ref,
    counts_ref,
    out_hbm,
    g_stage,
    g_high,
    g_low,
    m_stage,
    pick_ref,
    wf_high,
    wf_low,
    wb_high,
    wb_low,
    wt_high,
    wt_low,
    q_ref,
    qt_ref,
    p_ref,
    d_ref,
    w_ref,
    y_ref,
    yp_ref,
    ym_ref,
    r_ref,
    sol_ref,
    msend,
    qsend,
    qrecv,
    *rest,
):
    sends, recvs = rest[:N_ROUND], rest[N_ROUND : 2 * N_ROUND]
    mrecv = rest[2 * N_ROUND : 2 * N_ROUND + N_HALO]
    (load_sem, out_sem, send_sem, recv_sem, self_sem, ms_sem, mr_sem, qs_sem, qr_sem, ready_sem) = rest[
        2 * N_ROUND + N_HALO :
    ]
    faces, dirs, length = p_ref.shape
    rows = m_stage.shape[0]
    modes = coarse_hbm.shape[0]
    slots = CAP * N_DEV
    org, sub = lax.axis_index("organ"), lax.axis_index("sub")
    me = org * N_SUB + sub
    x_at, core_at, z_at, y_at = org // 2, org % 2, sub // 4, sub % 4

    organs = [
        ((x_at + dx) % 4) * 2 + (core_at + dc) % 2 for dx in (2, 3, 1, 0) for dc in (1, 0)
    ]

    def each_peer(visit):
        def subs(i, carry):
            z_to = (z_at + offset_of(3 - i // 4)) % 4
            y_to = (y_at + offset_of(3 - i % 4)) % 4
            for o in organs:
                visit(o, z_to * 4 + y_to)
            return carry

        lax.fori_loop(0, N_SUB - 1, subs, 0)
        for o in organs[:-1]:
            visit(o, sub)

    barrier = pltpu.get_barrier_semaphore()
    for i in range(N_SUB - 1):
        to = ((z_at + (2, 3, 1, 0)[i // 4]) % 4) * 4 + (y_at + (2, 3, 1, 0)[i % 4]) % 4
        pl.semaphore_signal(barrier, inc=1, device_id=(org, to), device_id_type=MESH)
    for o in organs[:-1]:
        pl.semaphore_signal(barrier, inc=1, device_id=(o, sub), device_id_type=MESH)

    loads = [pltpu.make_async_copy(mortar_hbm, m_stage, load_sem.at[0])]
    q_ref[...] = jnp.zeros(q_ref.shape, F32)
    qt_ref[...] = jnp.zeros(qt_ref.shape, F32)
    q_loads = [
        pltpu.make_async_copy(
            coarse_hbm.at[:, f, 0], q_ref.at[f, pl.ds(0, modes)], load_sem.at[1 + f]
        )
        for f in range(faces)
    ]
    x_loads = [
        pltpu.make_async_copy(warm_hbm.at[:, f, 0], p_ref.at[f], load_sem.at[6 + f])
        for f in range(faces)
    ]
    r_loads = [
        pltpu.make_async_copy(rhs_hbm.at[:, f, 0], r_ref.at[f], load_sem.at[11 + f])
        for f in range(faces)
    ]
    g_loads = [
        pltpu.make_async_copy(inv_hbm.at[f], g_stage.at[f], load_sem.at[16 + f])
        for f in range(faces)
    ]
    for copy in q_loads + loads + r_loads + x_loads + g_loads:
        copy.start()

    def start_round(i):
        n = ROWS[i]
        sb, rb = sends[i], recvs[i]

        def send(o, s):
            pltpu.make_async_remote_copy(
                sb.at[pl.ds((o * N_SUB + s) * n, n)],
                rb.at[pl.ds(me * n, n)],
                send_sem.at[i],
                recv_sem.at[i],
                device_id=(o, s),
                device_id_type=MESH,
            ).start()

        each_peer(send)
        pltpu.make_async_copy(
            sb.at[pl.ds(me * n, n)], rb.at[pl.ds(me * n, n)], self_sem.at[i]
        ).start()

    def wait_round(i):
        n = ROWS[i]
        sb, rb = sends[i], recvs[i]
        pltpu.make_async_copy(
            sb.at[pl.ds(me * n, n)], rb.at[pl.ds(me * n, n)], self_sem.at[i]
        ).wait()
        most = pl.ds(0, (N_DEV - 1) * n)
        pltpu.make_async_copy(rb.at[most], rb.at[most], recv_sem.at[i]).wait()
        pltpu.make_async_copy(sb.at[most], sb.at[most], send_sem.at[i]).wait()

    def put(i, j, value):
        sends[i][pl.ds(j, N_DEV, stride=ROWS[i]), :] = value

    def got(i, j):
        return recvs[i][pl.ds(j, N_DEV, stride=ROWS[i]), :]

    def partners():
        out = []
        for r in range(3):
            step = 2**r
            out.append((org, sub + step * (1 - 2 * ((sub // step) % 2))))
        for r in range(2):
            step = 2**r
            out.append((org + step * (1 - 2 * ((org // step) % 2)), sub))
        return out

    face_of = [rounds_ref[0, r] for r in range(N_MATCH)]
    round_of = []
    for f in range(faces):
        found = jnp.int32(0)
        for r in range(1, N_MATCH):
            found = jnp.where(face_of[r] == f, r, found)
        round_of.append(found)

    def start_match(source, send, recv, s_sem, r_sem):
        copies = []
        for r, dev in enumerate(partners()):
            send[r] = source[face_of[r]]
        for r, dev in enumerate(partners()):
            copy = pltpu.make_async_remote_copy(
                send.at[r], recv.at[r], s_sem.at[r], r_sem.at[r], device_id=dev, device_id_type=MESH
            )
            copy.start()
            copies.append(copy)
        return copies

    live = (active_ref[...] > 0) & (iota((1, rows), 1) < counts_ref[0, 0])
    owner = jnp.where(live, owner_ref[...], -1)
    owned = iota((N_DEV, rows), 0) == owner
    before = (iota((rows, rows), 0) < iota((rows, rows), 1)).astype(F32).astype(BF16)
    earlier = dot(owned.astype(F32).astype(BF16), before)
    rank = jnp.sum(jnp.where(owned, earlier, 0.0), axis=0, keepdims=True).astype(jnp.int32)
    slot = jnp.where(live, rank * N_DEV + owner, -1)
    dof_plus = dofs_ref[...].astype(F32) + 1.0
    lane = iota((N_DEV, LANES), 1)
    table = jnp.zeros((N_DEV, LANES), F32)
    for k in range(CAP):
        chosen = iota((N_DEV, rows), 0) + k * N_DEV == slot
        pick_ref[k] = chosen.astype(F32).astype(BF16)
        column = jnp.sum(jnp.where(chosen, dof_plus, 0.0), axis=1, keepdims=True) - 1.0
        table = jnp.where(lane == k, column, table)

    for copy in q_loads:
        copy.wait()
    gram = jnp.zeros((8, LANES), F32)
    for f in range(faces):
        own = q_ref[f, :8]
        tiled = jnp.concatenate([own] * (LANES // 8), axis=0)
        gram = gram + lax.dot_general(
            own, tiled, (((1,), (1,)), ((), ())), precision=lax.Precision.HIGHEST,
            preferred_element_type=F32,
        )
    keep = iota((8, LANES), 1) // 8 == iota((8, LANES), 0) + 8
    table = table + jnp.sum(jnp.where(keep, gram, 0.0), axis=0, keepdims=True)
    put(0, 0, table)
    pl.semaphore_wait(barrier, N_SUB + N_ORG - 2)
    for o in organs[:-1]:
        pl.semaphore_signal(ready_sem, inc=1, device_id=(o, sub), device_id_type=MESH)
    pl.semaphore_wait(ready_sem, N_ORG - 1)
    start_round(0)

    for copy in loads:
        copy.wait()
    m_high, m_low = split2(m_stage[...])

    def arrange(k, carry):
        at = pl.ds(pl.multiple_of(k * N_DEV, N_DEV), N_DEV)
        for part, back, ahead in ((m_high, wb_high, wf_high), (m_low, wb_low, wf_low)):
            block = dot(pick_ref[k], part).astype(BF16)
            back[at, :] = block
            ahead[:, at] = block.T
        return carry

    lax.fori_loop(0, CAP, arrange, 0)

    eye = [iota((dirs, LANES), 1) == iota((dirs, LANES), 0) + dirs * m for m in range(8)]

    def to_row(columns):
        total = jnp.zeros((dirs, LANES), F32)
        for m, column in columns:
            total = total + jnp.where(eye[m], column, 0.0)
        return jnp.sum(total, axis=0, keepdims=True)

    def to_column(row, m):
        return jnp.sum(jnp.where(eye[m], row, 0.0), axis=1, keepdims=True)

    def inner(a_ref, b_ref):
        total = a_ref[0] * b_ref[0]
        for f in range(1, faces):
            total = total + a_ref[f] * b_ref[f]
        return jnp.sum(total, axis=1, keepdims=True)

    for copy in r_loads:
        copy.wait()
    rhs_modes = []
    for m in range(modes):
        total = r_ref[0] * q_ref[0, m : m + 1]
        for f in range(1, faces):
            total = total + r_ref[f] * q_ref[f, m : m + 1]
        rhs_modes.append((m, jnp.sum(total, axis=1, keepdims=True)))
    rhs_row = to_row(rhs_modes)

    for copy in x_loads:
        copy.wait()
    copies = start_match(p_ref, msend.at[0], mrecv[0], ms_sem.at[0], mr_sem.at[0])
    for r in range(N_MATCH):
        qsend[r] = q_ref[face_of[r], :8]
    q_copies = []
    for r, dev in enumerate(partners()):
        copy = pltpu.make_async_remote_copy(
            qsend.at[r], qrecv.at[r], qs_sem.at[r], qr_sem.at[r], device_id=dev, device_id_type=MESH
        )
        copy.start()
        q_copies.append(copy)

    wait_round(0)
    table = recvs[0][...]
    table_t = table.T
    in_group = iota((N_DEV, LANES), 0) // N_SUB == org
    gram_row = jnp.sum(jnp.where(in_group, table, 0.0), axis=0, keepdims=True)
    for k in range(CAP):
        hit = iota((length, N_DEV), 0) == table_t[k : k + 1, :].astype(jnp.int32)
        wf_high[:, slots + k * N_DEV : slots + (k + 1) * N_DEV] = jnp.where(hit, 1.0, 0.0).astype(BF16)

    def row_values(x):
        n = x.shape[0]
        high, low = split2(x)
        full = dot(jnp.concatenate([high, low], axis=0), wf_high[...])
        full = full[:n] + full[n:]
        return full[:, :slots] + dot(high, wf_low[...]), full[:, slots:]

    def spread_gaps(gaps):
        n = gaps.shape[0]
        high, low = split2(gaps)
        full = dot(jnp.concatenate([high, low], axis=0), wb_high[...])
        return full[:n] + (full[n:] + dot(high[:, :slots], wb_low[...]))

    def stacked(value):
        return jnp.concatenate(
            [value[:, k * N_DEV : (k + 1) * N_DEV] for k in range(CAP)], axis=0
        )

    def unstacked(value):
        n = value.shape[0] // CAP
        return jnp.concatenate([value[k * n : (k + 1) * n] for k in range(CAP)], axis=1)

    def face_gaps(i, mine_a, mine_s):
        theirs_a, theirs_s = got(i, 0).T, got(i, 1).T
        return jnp.concatenate(
            [unstacked(mine_a - theirs_s), unstacked(theirs_a - mine_s)], axis=1
        )

    both_a, both_s = row_values(jnp.concatenate([p_ref[0], q_ref[0]], axis=0))
    mine_a, mine_s = stacked(both_a[:dirs]), stacked(both_s[:dirs])
    qa, qs = both_a[dirs : dirs + 8], both_s[dirs : dirs + 8]
    put(1, 0, mine_a.T)
    put(1, 1, mine_s.T)
    put(1, 2, jnp.broadcast_to(rhs_row, (N_DEV, LANES)))
    put(1, 3, jnp.concatenate([stacked(qa), stacked(qs)], axis=0).T)
    start_round(1)

    for k in range(CAP):
        column = table[:, k : k + 1].astype(jnp.int32)
        hit = iota((N_DEV, length), 1) == column
        wb_high[slots + k * N_DEV : slots + (k + 1) * N_DEV, :] = jnp.where(hit, -1.0, 0.0).astype(BF16)

    def gram_at(i, j):
        at = 64 + 8 * i + j
        return gram_row[:, at : at + 1]

    factor, inverse = {}, []
    for j in range(modes):
        pivot = gram_at(j, j)
        for k in range(j):
            pivot = pivot - factor[j, k] * factor[j, k]
        pivot = jnp.sqrt(pivot)
        inverse.append(1.0 / pivot)
        for i in range(j + 1, modes):
            value = gram_at(i, j)
            for k in range(j):
                value = value - factor[i, k] * factor[j, k]
            factor[i, j] = value * inverse[j]
    for f in range(faces):
        made = []
        for i in range(modes):
            row = q_ref[f, i : i + 1]
            for k in range(i):
                row = row - factor[i, k] * made[k]
            made.append(row * inverse[i])
            qt_ref[f, i : i + 1] = made[i]

    chunk = 64
    for f in range(faces):
        g_loads[f].wait()

        def halve(i, carry, f=f):
            at = pl.ds(pl.multiple_of(i * chunk, chunk), chunk)
            high, low = split2(g_stage[f, at, :])
            g_high[f, at, :] = high
            g_low[f, at, :] = low
            return carry

        lax.fori_loop(0, length // chunk, halve, 0)

    def make_wide(f, extra):
        at_round = round_of[f]
        other = jnp.where(
            at_round < 3,
            org,
            jnp.where(at_round == 3, org + 1 - 2 * (org % 2), org + 2 - 4 * ((org // 2) % 2)),
        )
        arrived = qrecv[at_round]
        organ_col = iota((8, length), 0)
        parts = []
        for m in range(modes):
            part = jnp.where(organ_col == org, q_ref[f, m : m + 1], 0.0) - jnp.where(
                organ_col == other, arrived[m : m + 1], 0.0
            )
            if extra is not None:
                part = part + extra[8 * m : 8 * m + 8]
            parts.append(part)
        parts.append(jnp.zeros((LANES - 8 * modes, length), F32))
        high, low = split2(jnp.concatenate(parts, axis=0).T)
        wt_high[f] = high
        wt_low[f] = low

    rho = None
    c_res = None
    coarse_rest = None
    for t in range(ITERS + 1):
        a_round = 1 + 2 * t
        for copy in copies:
            copy.wait()
        halo = mrecv[2 * t]
        for f in range(faces):
            yp_ref[f] = p_ref[f] - halo[round_of[f]]

        def smooth_face(f, carry):
            ym_ref[f] = mm(
                yp_ref[f], g_high[f], g_low[f]
            )
            return carry

        lax.fori_loop(1, faces, smooth_face, 0)
        if t == 0:
            for copy in q_copies:
                copy.wait()
            for f in range(1, faces):
                make_wide(f, None)
        if t < ITERS:
            coarse_part = mm(ym_ref[1], wt_high[1], wt_low[1])
            for f in range(2, faces):
                coarse_part = coarse_part + mm(ym_ref[f], wt_high[f], wt_low[f])

        wait_round(a_round)
        gaps = face_gaps(a_round, mine_a, mine_s)
        if t == 0:
            c_row = jnp.sum(jnp.where(in_group, got(1, 2), 0.0), axis=0, keepdims=True)
            c_res = [to_column(c_row, m) for m in range(modes)]
            theirs = got(1, 3).T
            organ_row = iota((8, LANES), 0)
            of_peer = iota((8, LANES), 1) // N_SUB == organ_row
            mine = organ_row == org
            blocks = []
            for m in range(modes):
                outs, ins = [], []
                for k in range(CAP):
                    at = slice(k * N_DEV, (k + 1) * N_DEV)
                    ta = theirs[k * 8 + m : k * 8 + m + 1]
                    ts = theirs[64 + k * 8 + m : 64 + k * 8 + m + 1]
                    outs.append(
                        jnp.where(mine, qa[m : m + 1, at], 0.0) - jnp.where(of_peer, ts, 0.0)
                    )
                    ins.append(
                        jnp.where(of_peer, ta, 0.0) - jnp.where(mine, qs[m : m + 1, at], 0.0)
                    )
                blocks.append(jnp.concatenate(outs + ins, axis=1))
            mode_gaps = jnp.concatenate(blocks, axis=0)
            both = spread_gaps(jnp.concatenate([gaps, mode_gaps], axis=0))
            contact, mode_contact = both[:dirs], both[dirs:]
            make_wide(0, mode_contact)
        else:
            contact = spread_gaps(gaps)
            rho_new = to_column(jnp.sum(got(a_round, 2), axis=0, keepdims=True), 0)
            beta = rho_new / rho if t > 1 else None
            rho = rho_new
        yp_ref[0] = yp_ref[0] + contact
        ym_ref[0] = mm(yp_ref[0], g_high[0], g_low[0])

        for f in range(faces):
            y_ref[f] = ym_ref[f] + beta * y_ref[f] if t > 1 else ym_ref[f]
        if t < ITERS:
            copies = start_match(
                y_ref,
                msend.at[2 * t + 1],
                mrecv[2 * t + 1],
                ms_sem.at[2 * t + 1],
                mr_sem.at[2 * t + 1],
            )
        for f in range(faces):
            if t > 1:
                w_ref[f] = yp_ref[f] + beta * w_ref[f]
                d_ref[f] = p_ref[f] + beta * d_ref[f]
            else:
                w_ref[f] = yp_ref[f]
                d_ref[f] = p_ref[f]
        curved = inner(w_ref, y_ref)

        b_round = a_round + 1
        if t == ITERS:
            put(b_round, 0, jnp.broadcast_to(to_row([(0, curved)]), (N_DEV, LANES)))
            start_round(b_round)
            wait_round(b_round)
            step = rho / to_column(jnp.sum(recvs[b_round][...], axis=0, keepdims=True), 0)
            for f in range(faces):
                sol_ref[f] = sol_ref[f] + step * d_ref[f]
            break

        mine_a, mine_s = row_values(y_ref[0])
        mine_a, mine_s = stacked(mine_a), stacked(mine_s)
        put(b_round, 0, mine_a.T)
        put(b_round, 1, mine_s.T)
        coarse_rest = coarse_part + beta * coarse_rest if t > 1 else coarse_part
        coarse = coarse_rest + mm(y_ref[0], wt_high[0], wt_low[0])
        coarse = jnp.concatenate([coarse, jnp.zeros((LANES - dirs, LANES), F32)], axis=0).T
        parts = [coarse[8 * m : 8 * m + 8, :dirs] for m in range(modes)]
        parts.append(jnp.zeros((8, LANES - modes * dirs), F32))
        coarse = jnp.concatenate(parts, axis=1) + to_row([(modes, curved)])
        for o in range(N_ORG):
            sends[b_round][pl.ds(o * N_SUB * ROWS[b_round] + 2, N_SUB, stride=ROWS[b_round]), :] = (
                jnp.broadcast_to(coarse[o : o + 1], (N_SUB, LANES))
            )
        start_round(b_round)

        for copy in copies:
            copy.wait()
        halo = mrecv[2 * t + 1]
        for f in range(faces):
            yp_ref[f] = y_ref[f] - halo[round_of[f]]
        wait_round(b_round)
        yp_ref[0] = yp_ref[0] + spread_gaps(face_gaps(b_round, mine_a, mine_s))
        total = jnp.sum(got(b_round, 2), axis=0, keepdims=True)
        c_image = [to_column(total, m) for m in range(modes)]
        if t > 0:
            step = rho / to_column(total, modes)
        for f in range(faces):
            if t > 0:
                r_ref[f] = r_ref[f] - step * yp_ref[f]
            else:
                r_ref[f] = r_ref[f] - yp_ref[f]
        for m in range(modes):
            c_res[m] = c_res[m] - (step * c_image[m] if t > 0 else c_image[m])
        solved = []
        for i in range(modes):
            value = c_res[i]
            for k in range(i):
                value = value - factor[i, k] * solved[k]
            solved.append(value * inverse[i])
        for f in range(faces):
            value = r_ref[f]
            for m in range(modes):
                value = value - solved[m] * qt_ref[f, m : m + 1]
            p_ref[f] = value

        n_halo = 2 * t + 2
        copies = start_match(
            p_ref, msend.at[n_halo], mrecv[n_halo], ms_sem.at[n_halo], mr_sem.at[n_halo]
        )
        for f in range(faces):
            sol_ref[f] = sol_ref[f] + step * d_ref[f] if t > 0 else d_ref[f]
        mine_a, mine_s = row_values(p_ref[0])
        mine_a, mine_s = stacked(mine_a), stacked(mine_s)
        put(b_round + 1, 0, mine_a.T)
        put(b_round + 1, 1, mine_s.T)
        put(
            b_round + 1,
            2,
            jnp.broadcast_to(to_row([(0, inner(r_ref, p_ref))]), (N_DEV, LANES)),
        )
        start_round(b_round + 1)

    writes = [
        pltpu.make_async_copy(sol_ref.at[f], out_hbm.at[:, f, 0], out_sem.at[f])
        for f in range(faces)
    ]
    for copy in writes:
        copy.start()
    for copy in writes:
        copy.wait()


def local(
    dual_rhs,
    warm_start,
    inverse_blocks,
    coarse_basis,
    mortar_rows,
    match_rounds,
    slave_owner,
    slave_dofs,
    active_set,
    row_counts,
):
    dirs, _, _, faces, length = dual_rhs.shape
    rows = mortar_rows.shape[2]
    modes = coarse_basis.shape[0]
    slots = CAP * N_DEV
    field = pltpu.VMEM((faces, dirs, length), F32)
    dma = pltpu.SemaphoreType.DMA
    any_spec = pl.BlockSpec(memory_space=pl.ANY)
    vmem_spec = pl.BlockSpec(memory_space=pltpu.VMEM)
    smem_spec = pl.BlockSpec(memory_space=pltpu.SMEM)
    scratch = [
        pltpu.VMEM((faces, length, length), F32),
        pltpu.VMEM((faces, length, length), BF16),
        pltpu.VMEM((faces, length, length), BF16),
        pltpu.VMEM((rows, length), F32),
        pltpu.VMEM((CAP, N_DEV, rows), BF16),
        pltpu.VMEM((length, 2 * slots), BF16),
        pltpu.VMEM((length, slots), BF16),
        pltpu.VMEM((2 * slots, length), BF16),
        pltpu.VMEM((slots, length), BF16),
        pltpu.VMEM((faces, length, LANES), BF16),
        pltpu.VMEM((faces, length, LANES), BF16),
        field,
        pltpu.VMEM((faces, 8, length), F32),
    ]
    scratch += [field] * 8
    scratch += [
        pltpu.VMEM((N_HALO, N_MATCH, dirs, length), F32),
        pltpu.VMEM((N_MATCH, 8, length), F32),
        pltpu.VMEM((N_MATCH, 8, length), F32),
    ]
    scratch += [pltpu.VMEM((N_DEV * n, LANES), F32) for n in ROWS] * 2
    scratch += [pltpu.VMEM((N_MATCH, dirs, length), F32)] * N_HALO
    scratch += [
        dma((21,)),
        dma((faces,)),
        dma((N_ROUND,)),
        dma((N_ROUND,)),
        dma((N_ROUND,)),
        dma((N_HALO, N_MATCH)),
        dma((N_HALO, N_MATCH)),
        dma((N_MATCH,)),
        dma((N_MATCH,)),
        pltpu.SemaphoreType.REGULAR,
    ]
    result = pl.pallas_call(
        kernel,
        out_shape=jax.ShapeDtypeStruct((dirs, faces, 1, length), F32),
        in_specs=[any_spec] * 5 + [vmem_spec] * 3 + [smem_spec] * 2,
        out_specs=any_spec,
        scratch_shapes=scratch,
        compiler_params=pltpu.CompilerParams(
            collective_id=0, has_side_effects=True, vmem_limit_bytes=60 * 2**20
        ),
    )(
        dual_rhs.reshape(dirs, faces, 1, length),
        warm_start.reshape(dirs, faces, 1, length),
        inverse_blocks.reshape(faces, length, length),
        coarse_basis.reshape(modes, faces, 1, length),
        mortar_rows.reshape(rows, length),
        slave_owner.reshape(1, rows),
        slave_dofs.reshape(1, rows),
        active_set.reshape(1, rows),
        match_rounds.reshape(1, N_MATCH),
        row_counts.reshape(1, 1),
    )
    return result.reshape(dirs, 1, 1, faces, length)


def solution(mesh):
    in_specs = (
        P(None, "organ", "sub", None, None),
        P(None, "organ", "sub", None, None),
        P("organ", "sub", None, None, None),
        P(None, "organ", "sub", None, None),
        P("organ", "sub", None, None),
        P("organ", "sub", None),
        P("organ", "sub", None, None),
        P("organ", "sub", None),
        P("organ", "sub", None),
        P("organ", "sub", None),
    )
    out_specs = P(None, "organ", "sub", None, None)
    return jax.shard_map(local, mesh=mesh, in_specs=in_specs, out_specs=out_specs, check_vma=False)
```

```python
import jax
import jax.numpy as jnp
from jax import lax
from jax.experimental import pallas as pl
from jax.experimental.pallas import tpu as pltpu
from jax.sharding import PartitionSpec as P

ITERS = 3
CAP = 8
MESH = pl.DeviceIdType.MESH
F32 = jnp.float32
BF16 = jnp.bfloat16
N_ORG, N_SUB = 8, 16
N_DEV = N_ORG * N_SUB
LANES = 128
ROWS = (1, 4, 3, 3, 3, 3, 3, 3, 1)
N_ROUND = len(ROWS)
N_MATCH = 5
N_HALO = 2 * ITERS + 1


def iota(shape, dim):
    return lax.broadcasted_iota(jnp.int32, shape, dim)


def split2(x):
    high = x.astype(BF16)
    return high, (x - high.astype(F32)).astype(BF16)


def dot(a, b):
    return jnp.dot(a, b, preferred_element_type=F32)


def mm(x, w_high, w_low):
    n = x.shape[0]
    high, low = split2(x)
    a = dot(jnp.concatenate([high, low], axis=0), w_high)
    return a[:n] + (a[n:] + dot(high, w_low))


def offset_of(u):
    return u - (u // 2) * (2 * u - 5)


def kernel(
    rhs_hbm,
    warm_hbm,
    inv_hbm,
    coarse_hbm,
    mortar_hbm,
    owner_ref,
    dofs_ref,
    active_ref,
    rounds_ref,
    counts_ref,
    out_hbm,
    g_stage,
    g_high,
    g_low,
    m_stage,
    pick_ref,
    wf_high,
    wf_low,
    wb_high,
    wb_low,
    wt_high,
    wt_low,
    q_ref,
    qt_ref,
    p_ref,
    d_ref,
    w_ref,
    y_ref,
    yp_ref,
    ym_ref,
    r_ref,
    sol_ref,
    msend,
    qsend,
    qrecv,
    *rest,
):
    sends, recvs = rest[:N_ROUND], rest[N_ROUND : 2 * N_ROUND]
    mrecv = rest[2 * N_ROUND : 2 * N_ROUND + N_HALO]
    (load_sem, out_sem, send_sem, recv_sem, self_sem, ms_sem, mr_sem, qs_sem, qr_sem, ready_sem) = rest[
        2 * N_ROUND + N_HALO :
    ]
    faces, dirs, length = p_ref.shape
    rows = m_stage.shape[0]
    modes = coarse_hbm.shape[0]
    slots = CAP * N_DEV
    org, sub = lax.axis_index("organ"), lax.axis_index("sub")
    me = org * N_SUB + sub
    x_at, core_at, z_at, y_at = org // 2, org % 2, sub // 4, sub % 4

    organs = [
        ((x_at + dx) % 4) * 2 + (core_at + dc) % 2 for dx in (2, 3, 1, 0) for dc in (1, 0)
    ]

    def each_peer(visit):
        def subs(i, digits):
            z_digits, y_digits = digits
            to = (z_at + z_digits % 4) % 4 * 4 + (y_at + y_digits % 4) % 4
            for o in organs:
                visit(o, to)
            return z_digits // 4, y_digits // 4

        order = sorted(
            [(z, y) for z in range(4) for y in range(4) if z or y],
            key=lambda at: -sum(min(d, 4 - d) for d in at),
        )
        z_all = sum(z * 4**i for i, (z, _) in enumerate(order))
        y_all = sum(y * 4**i for i, (_, y) in enumerate(order))
        lax.fori_loop(0, N_SUB - 1, subs, (jnp.int32(z_all), jnp.int32(y_all)))
        for o in organs[:-1]:
            visit(o, sub)

    barrier = pltpu.get_barrier_semaphore()
    for i in range(N_SUB - 1):
        to = ((z_at + (2, 3, 1, 0)[i // 4]) % 4) * 4 + (y_at + (2, 3, 1, 0)[i % 4]) % 4
        pl.semaphore_signal(barrier, inc=1, device_id=(org, to), device_id_type=MESH)
    for o in organs[:-1]:
        pl.semaphore_signal(barrier, inc=1, device_id=(o, sub), device_id_type=MESH)

    loads = [pltpu.make_async_copy(mortar_hbm, m_stage, load_sem.at[0])]
    q_ref[...] = jnp.zeros(q_ref.shape, F32)
    qt_ref[...] = jnp.zeros(qt_ref.shape, F32)
    q_loads = [
        pltpu.make_async_copy(
            coarse_hbm.at[:, f, 0], q_ref.at[f, pl.ds(0, modes)], load_sem.at[1 + f]
        )
        for f in range(faces)
    ]
    x_loads = [
        pltpu.make_async_copy(warm_hbm.at[:, f, 0], p_ref.at[f], load_sem.at[6 + f])
        for f in range(faces)
    ]
    r_loads = [
        pltpu.make_async_copy(rhs_hbm.at[:, f, 0], r_ref.at[f], load_sem.at[11 + f])
        for f in range(faces)
    ]
    g_loads = [
        pltpu.make_async_copy(inv_hbm.at[f], g_stage.at[f], load_sem.at[16 + f])
        for f in range(faces)
    ]
    for copy in q_loads + loads + r_loads + x_loads + g_loads:
        copy.start()

    def start_round(i):
        n = ROWS[i]
        sb, rb = sends[i], recvs[i]

        def send(o, s):
            pltpu.make_async_remote_copy(
                sb.at[pl.ds((o * N_SUB + s) * n, n)],
                rb.at[pl.ds(me * n, n)],
                send_sem.at[i],
                recv_sem.at[i],
                device_id=(o, s),
                device_id_type=MESH,
            ).start()

        each_peer(send)
        pltpu.make_async_copy(
            sb.at[pl.ds(me * n, n)], rb.at[pl.ds(me * n, n)], self_sem.at[i]
        ).start()

    def wait_round(i):
        n = ROWS[i]
        sb, rb = sends[i], recvs[i]
        pltpu.make_async_copy(
            sb.at[pl.ds(me * n, n)], rb.at[pl.ds(me * n, n)], self_sem.at[i]
        ).wait()
        most = pl.ds(0, (N_DEV - 1) * n)
        pltpu.make_async_copy(rb.at[most], rb.at[most], recv_sem.at[i]).wait()
        pltpu.make_async_copy(sb.at[most], sb.at[most], send_sem.at[i]).wait()

    def put(i, j, value):
        sends[i][pl.ds(j, N_DEV, stride=ROWS[i]), :] = value

    def got(i, j):
        return recvs[i][pl.ds(j, N_DEV, stride=ROWS[i]), :]

    def partners():
        out = []
        for r in range(3):
            step = 2**r
            out.append((org, sub + step * (1 - 2 * ((sub // step) % 2))))
        for r in range(2):
            step = 2**r
            out.append((org + step * (1 - 2 * ((org // step) % 2)), sub))
        return out

    face_of = [rounds_ref[0, r] for r in range(N_MATCH)]
    round_of = []
    for f in range(faces):
        found = jnp.int32(0)
        for r in range(1, N_MATCH):
            found = jnp.where(face_of[r] == f, r, found)
        round_of.append(found)

    def start_match(source, send, recv, s_sem, r_sem):
        copies = []
        for r, dev in enumerate(partners()):
            send[r] = source[face_of[r]]
        devices = partners()
        for r in (1, 0, 2, 4, 3):
            dev = devices[r]
            copy = pltpu.make_async_remote_copy(
                send.at[r], recv.at[r], s_sem.at[r], r_sem.at[r], device_id=dev, device_id_type=MESH
            )
            copy.start()
            copies.append(copy)
        return copies

    live = (active_ref[...] > 0) & (iota((1, rows), 1) < counts_ref[0, 0])
    owner = jnp.where(live, owner_ref[...], -1)
    owned = iota((N_DEV, rows), 0) == owner
    before = (iota((rows, rows), 0) < iota((rows, rows), 1)).astype(F32).astype(BF16)
    earlier = dot(owned.astype(F32).astype(BF16), before)
    rank = jnp.sum(jnp.where(owned, earlier, 0.0), axis=0, keepdims=True).astype(jnp.int32)
    slot = jnp.where(live, rank * N_DEV + owner, -1)
    dof_plus = dofs_ref[...].astype(F32) + 1.0
    lane = iota((N_DEV, LANES), 1)
    table = jnp.zeros((N_DEV, LANES), F32)
    for k in range(CAP):
        chosen = iota((N_DEV, rows), 0) + k * N_DEV == slot
        pick_ref[k] = chosen.astype(F32).astype(BF16)
        column = jnp.sum(jnp.where(chosen, dof_plus, 0.0), axis=1, keepdims=True) - 1.0
        table = jnp.where(lane == k, column, table)

    for copy in q_loads:
        copy.wait()
    gram = jnp.zeros((8, LANES), F32)
    for f in range(faces):
        own = q_ref[f, :8]
        tiled = jnp.concatenate([own] * (LANES // 8), axis=0)
        gram = gram + lax.dot_general(
            own, tiled, (((1,), (1,)), ((), ())), precision=lax.Precision.HIGHEST,
            preferred_element_type=F32,
        )
    keep = iota((8, LANES), 1) // 8 == iota((8, LANES), 0) + 8
    table = table + jnp.sum(jnp.where(keep, gram, 0.0), axis=0, keepdims=True)
    put(0, 0, table)
    pl.semaphore_wait(barrier, N_SUB + N_ORG - 2)
    for o in organs[:-1]:
        pl.semaphore_signal(ready_sem, inc=1, device_id=(o, sub), device_id_type=MESH)
    pl.semaphore_wait(ready_sem, N_ORG - 1)
    start_round(0)

    for copy in loads:
        copy.wait()
    m_high, m_low = split2(m_stage[...])

    def arrange(k, carry):
        at = pl.ds(pl.multiple_of(k * N_DEV, N_DEV), N_DEV)
        for part, back, ahead in ((m_high, wb_high, wf_high), (m_low, wb_low, wf_low)):
            block = dot(pick_ref[k], part).astype(BF16)
            back[at, :] = block
            ahead[:, at] = block.T
        return carry

    lax.fori_loop(0, CAP, arrange, 0)

    eye = [iota((dirs, LANES), 1) == iota((dirs, LANES), 0) + dirs * m for m in range(8)]

    def to_row(columns):
        total = jnp.zeros((dirs, LANES), F32)
        for m, column in columns:
            total = total + jnp.where(eye[m], column, 0.0)
        return jnp.sum(total, axis=0, keepdims=True)

    def to_column(row, m):
        return jnp.sum(jnp.where(eye[m], row, 0.0), axis=1, keepdims=True)

    def inner(a_ref, b_ref):
        total = a_ref[0] * b_ref[0]
        for f in range(1, faces):
            total = total + a_ref[f] * b_ref[f]
        return jnp.sum(total, axis=1, keepdims=True)

    for copy in r_loads:
        copy.wait()
    rhs_modes = []
    for m in range(modes):
        total = r_ref[0] * q_ref[0, m : m + 1]
        for f in range(1, faces):
            total = total + r_ref[f] * q_ref[f, m : m + 1]
        rhs_modes.append((m, jnp.sum(total, axis=1, keepdims=True)))
    rhs_row = to_row(rhs_modes)

    for copy in x_loads:
        copy.wait()
    copies = start_match(p_ref, msend.at[0], mrecv[0], ms_sem.at[0], mr_sem.at[0])
    for r in range(N_MATCH):
        qsend[r] = q_ref[face_of[r], :8]
    q_copies = []
    for r, dev in enumerate(partners()):
        copy = pltpu.make_async_remote_copy(
            qsend.at[r], qrecv.at[r], qs_sem.at[r], qr_sem.at[r], device_id=dev, device_id_type=MESH
        )
        copy.start()
        q_copies.append(copy)

    wait_round(0)
    table = recvs[0][...]
    table_t = table.T
    in_group = iota((N_DEV, LANES), 0) // N_SUB == org
    gram_row = jnp.sum(jnp.where(in_group, table, 0.0), axis=0, keepdims=True)
    for k in range(CAP):
        hit = iota((length, N_DEV), 0) == table_t[k : k + 1, :].astype(jnp.int32)
        wf_high[:, slots + k * N_DEV : slots + (k + 1) * N_DEV] = jnp.where(hit, 1.0, 0.0).astype(BF16)

    def row_values(x):
        n = x.shape[0]
        high, low = split2(x)
        full = dot(jnp.concatenate([high, low], axis=0), wf_high[...])
        full = full[:n] + full[n:]
        return full[:, :slots] + dot(high, wf_low[...]), full[:, slots:]

    def spread_gaps(gaps):
        n = gaps.shape[0]
        high, low = split2(gaps)
        full = dot(jnp.concatenate([high, low], axis=0), wb_high[...])
        return full[:n] + (full[n:] + dot(high[:, :slots], wb_low[...]))

    def stacked(value):
        return jnp.concatenate(
            [value[:, k * N_DEV : (k + 1) * N_DEV] for k in range(CAP)], axis=0
        )

    def unstacked(value):
        n = value.shape[0] // CAP
        return jnp.concatenate([value[k * n : (k + 1) * n] for k in range(CAP)], axis=1)

    def face_gaps(i, mine_a, mine_s):
        theirs_a, theirs_s = got(i, 0).T, got(i, 1).T
        return jnp.concatenate(
            [unstacked(mine_a - theirs_s), unstacked(theirs_a - mine_s)], axis=1
        )

    both_a, both_s = row_values(jnp.concatenate([p_ref[0], q_ref[0]], axis=0))
    mine_a, mine_s = stacked(both_a[:dirs]), stacked(both_s[:dirs])
    qa, qs = both_a[dirs : dirs + 8], both_s[dirs : dirs + 8]
    put(1, 0, mine_a.T)
    put(1, 1, mine_s.T)
    put(1, 2, jnp.broadcast_to(rhs_row, (N_DEV, LANES)))
    put(1, 3, jnp.concatenate([stacked(qa), stacked(qs)], axis=0).T)
    start_round(1)

    for k in range(CAP):
        column = table[:, k : k + 1].astype(jnp.int32)
        hit = iota((N_DEV, length), 1) == column
        wb_high[slots + k * N_DEV : slots + (k + 1) * N_DEV, :] = jnp.where(hit, -1.0, 0.0).astype(BF16)

    def gram_at(i, j):
        at = 64 + 8 * i + j
        return gram_row[:, at : at + 1]

    factor, inverse = {}, []
    for j in range(modes):
        pivot = gram_at(j, j)
        for k in range(j):
            pivot = pivot - factor[j, k] * factor[j, k]
        pivot = jnp.sqrt(pivot)
        inverse.append(1.0 / pivot)
        for i in range(j + 1, modes):
            value = gram_at(i, j)
            for k in range(j):
                value = value - factor[i, k] * factor[j, k]
            factor[i, j] = value * inverse[j]
    for f in range(faces):
        made = []
        for i in range(modes):
            row = q_ref[f, i : i + 1]
            for k in range(i):
                row = row - factor[i, k] * made[k]
            made.append(row * inverse[i])
            qt_ref[f, i : i + 1] = made[i]

    chunk = 64
    for f in range(faces):
        g_loads[f].wait()

        def halve(i, carry, f=f):
            at = pl.ds(pl.multiple_of(i * chunk, chunk), chunk)
            high, low = split2(g_stage[f, at, :])
            g_high[f, at, :] = high
            g_low[f, at, :] = low
            return carry

        lax.fori_loop(0, length // chunk, halve, 0)

    def make_wide(f, extra):
        at_round = round_of[f]
        other = jnp.where(
            at_round < 3,
            org,
            jnp.where(at_round == 3, org + 1 - 2 * (org % 2), org + 2 - 4 * ((org // 2) % 2)),
        )
        arrived = qrecv[at_round]
        organ_col = iota((8, length), 0)
        parts = []
        for m in range(modes):
            part = jnp.where(organ_col == org, q_ref[f, m : m + 1], 0.0) - jnp.where(
                organ_col == other, arrived[m : m + 1], 0.0
            )
            if extra is not None:
                part = part + extra[8 * m : 8 * m + 8]
            parts.append(part)
        parts.append(jnp.zeros((LANES - 8 * modes, length), F32))
        high, low = split2(jnp.concatenate(parts, axis=0).T)
        wt_high[f] = high
        wt_low[f] = low

    rho = None
    c_res = None
    coarse_rest = None
    for t in range(ITERS + 1):
        a_round = 1 + 2 * t
        for copy in copies:
            copy.wait()
        halo = mrecv[2 * t]
        for f in range(faces):
            yp_ref[f] = p_ref[f] - halo[round_of[f]]

        def smooth_face(f, carry):
            ym_ref[f] = mm(
                yp_ref[f], g_high[f], g_low[f]
            )
            return carry

        lax.fori_loop(1, faces, smooth_face, 0)
        if t == 0:
            for copy in q_copies:
                copy.wait()
            for f in range(1, faces):
                make_wide(f, None)
        if t < ITERS:
            coarse_part = mm(ym_ref[1], wt_high[1], wt_low[1])
            for f in range(2, faces):
                coarse_part = coarse_part + mm(ym_ref[f], wt_high[f], wt_low[f])

        wait_round(a_round)
        gaps = face_gaps(a_round, mine_a, mine_s)
        if t == 0:
            c_row = jnp.sum(jnp.where(in_group, got(1, 2), 0.0), axis=0, keepdims=True)
            c_res = [to_column(c_row, m) for m in range(modes)]
            theirs = got(1, 3).T
            organ_row = iota((8, LANES), 0)
            of_peer = iota((8, LANES), 1) // N_SUB == organ_row
            mine = organ_row == org
            blocks = []
            for m in range(modes):
                outs, ins = [], []
                for k in range(CAP):
                    at = slice(k * N_DEV, (k + 1) * N_DEV)
                    ta = theirs[k * 8 + m : k * 8 + m + 1]
                    ts = theirs[64 + k * 8 + m : 64 + k * 8 + m + 1]
                    outs.append(
                        jnp.where(mine, qa[m : m + 1, at], 0.0) - jnp.where(of_peer, ts, 0.0)
                    )
                    ins.append(
                        jnp.where(of_peer, ta, 0.0) - jnp.where(mine, qs[m : m + 1, at], 0.0)
                    )
                blocks.append(jnp.concatenate(outs + ins, axis=1))
            mode_gaps = jnp.concatenate(blocks, axis=0)
            both = spread_gaps(jnp.concatenate([gaps, mode_gaps], axis=0))
            contact, mode_contact = both[:dirs], both[dirs:]
            make_wide(0, mode_contact)
        else:
            contact = spread_gaps(gaps)
            rho_new = to_column(jnp.sum(got(a_round, 2), axis=0, keepdims=True), 0)
            beta = rho_new / rho if t > 1 else None
            rho = rho_new
        yp_ref[0] = yp_ref[0] + contact
        ym_ref[0] = mm(yp_ref[0], g_high[0], g_low[0])

        for f in range(faces):
            y_ref[f] = ym_ref[f] + beta * y_ref[f] if t > 1 else ym_ref[f]
        if t < ITERS:
            copies = start_match(
                y_ref,
                msend.at[2 * t + 1],
                mrecv[2 * t + 1],
                ms_sem.at[2 * t + 1],
                mr_sem.at[2 * t + 1],
            )
        for f in range(faces):
            if t > 1:
                w_ref[f] = yp_ref[f] + beta * w_ref[f]
                d_ref[f] = p_ref[f] + beta * d_ref[f]
            else:
                w_ref[f] = yp_ref[f]
                d_ref[f] = p_ref[f]
        curved = inner(w_ref, y_ref)

        b_round = a_round + 1
        if t == ITERS:
            put(b_round, 0, jnp.broadcast_to(to_row([(0, curved)]), (N_DEV, LANES)))
            start_round(b_round)
            wait_round(b_round)
            step = rho / to_column(jnp.sum(recvs[b_round][...], axis=0, keepdims=True), 0)
            for f in range(faces):
                sol_ref[f] = sol_ref[f] + step * d_ref[f]
            break

        mine_a, mine_s = row_values(y_ref[0])
        mine_a, mine_s = stacked(mine_a), stacked(mine_s)
        put(b_round, 0, mine_a.T)
        put(b_round, 1, mine_s.T)
        coarse_rest = coarse_part + beta * coarse_rest if t > 1 else coarse_part
        coarse = coarse_rest + mm(y_ref[0], wt_high[0], wt_low[0])
        coarse = jnp.concatenate([coarse, jnp.zeros((LANES - dirs, LANES), F32)], axis=0).T
        parts = [coarse[8 * m : 8 * m + 8, :dirs] for m in range(modes)]
        parts.append(jnp.zeros((8, LANES - modes * dirs), F32))
        coarse = jnp.concatenate(parts, axis=1) + to_row([(modes, curved)])
        for o in range(N_ORG):
            sends[b_round][pl.ds(o * N_SUB * ROWS[b_round] + 2, N_SUB, stride=ROWS[b_round]), :] = (
                jnp.broadcast_to(coarse[o : o + 1], (N_SUB, LANES))
            )
        start_round(b_round)

        for copy in copies:
            copy.wait()
        halo = mrecv[2 * t + 1]
        for f in range(faces):
            yp_ref[f] = y_ref[f] - halo[round_of[f]]
        wait_round(b_round)
        yp_ref[0] = yp_ref[0] + spread_gaps(face_gaps(b_round, mine_a, mine_s))
        total = jnp.sum(got(b_round, 2), axis=0, keepdims=True)
        c_image = [to_column(total, m) for m in range(modes)]
        if t > 0:
            step = rho / to_column(total, modes)
        for f in range(faces):
            if t > 0:
                r_ref[f] = r_ref[f] - step * yp_ref[f]
            else:
                r_ref[f] = r_ref[f] - yp_ref[f]
        for m in range(modes):
            c_res[m] = c_res[m] - (step * c_image[m] if t > 0 else c_image[m])
        solved = []
        for i in range(modes):
            value = c_res[i]
            for k in range(i):
                value = value - factor[i, k] * solved[k]
            solved.append(value * inverse[i])
        for f in range(faces):
            value = r_ref[f]
            for m in range(modes):
                value = value - solved[m] * qt_ref[f, m : m + 1]
            p_ref[f] = value

        n_halo = 2 * t + 2
        copies = start_match(
            p_ref, msend.at[n_halo], mrecv[n_halo], ms_sem.at[n_halo], mr_sem.at[n_halo]
        )
        for f in range(faces):
            sol_ref[f] = sol_ref[f] + step * d_ref[f] if t > 0 else d_ref[f]
        mine_a, mine_s = row_values(p_ref[0])
        mine_a, mine_s = stacked(mine_a), stacked(mine_s)
        put(b_round + 1, 0, mine_a.T)
        put(b_round + 1, 1, mine_s.T)
        put(
            b_round + 1,
            2,
            jnp.broadcast_to(to_row([(0, inner(r_ref, p_ref))]), (N_DEV, LANES)),
        )
        start_round(b_round + 1)

    writes = [
        pltpu.make_async_copy(sol_ref.at[f], out_hbm.at[:, f, 0], out_sem.at[f])
        for f in range(faces)
    ]
    for copy in writes:
        copy.start()
    for copy in writes:
        copy.wait()


def local(
    dual_rhs,
    warm_start,
    inverse_blocks,
    coarse_basis,
    mortar_rows,
    match_rounds,
    slave_owner,
    slave_dofs,
    active_set,
    row_counts,
):
    dirs, _, _, faces, length = dual_rhs.shape
    rows = mortar_rows.shape[2]
    modes = coarse_basis.shape[0]
    slots = CAP * N_DEV
    field = pltpu.VMEM((faces, dirs, length), F32)
    dma = pltpu.SemaphoreType.DMA
    any_spec = pl.BlockSpec(memory_space=pl.ANY)
    vmem_spec = pl.BlockSpec(memory_space=pltpu.VMEM)
    smem_spec = pl.BlockSpec(memory_space=pltpu.SMEM)
    scratch = [
        pltpu.VMEM((faces, length, length), F32),
        pltpu.VMEM((faces, length, length), BF16),
        pltpu.VMEM((faces, length, length), BF16),
        pltpu.VMEM((rows, length), F32),
        pltpu.VMEM((CAP, N_DEV, rows), BF16),
        pltpu.VMEM((length, 2 * slots), BF16),
        pltpu.VMEM((length, slots), BF16),
        pltpu.VMEM((2 * slots, length), BF16),
        pltpu.VMEM((slots, length), BF16),
        pltpu.VMEM((faces, length, LANES), BF16),
        pltpu.VMEM((faces, length, LANES), BF16),
        field,
        pltpu.VMEM((faces, 8, length), F32),
    ]
    scratch += [field] * 8
    scratch += [
        pltpu.VMEM((N_HALO, N_MATCH, dirs, length), F32),
        pltpu.VMEM((N_MATCH, 8, length), F32),
        pltpu.VMEM((N_MATCH, 8, length), F32),
    ]
    scratch += [pltpu.VMEM((N_DEV * n, LANES), F32) for n in ROWS] * 2
    scratch += [pltpu.VMEM((N_MATCH, dirs, length), F32)] * N_HALO
    scratch += [
        dma((21,)),
        dma((faces,)),
        dma((N_ROUND,)),
        dma((N_ROUND,)),
        dma((N_ROUND,)),
        dma((N_HALO, N_MATCH)),
        dma((N_HALO, N_MATCH)),
        dma((N_MATCH,)),
        dma((N_MATCH,)),
        pltpu.SemaphoreType.REGULAR,
    ]
    result = pl.pallas_call(
        kernel,
        out_shape=jax.ShapeDtypeStruct((dirs, faces, 1, length), F32),
        in_specs=[any_spec] * 5 + [vmem_spec] * 3 + [smem_spec] * 2,
        out_specs=any_spec,
        scratch_shapes=scratch,
        compiler_params=pltpu.CompilerParams(
            collective_id=0, has_side_effects=True, vmem_limit_bytes=60 * 2**20
        ),
    )(
        dual_rhs.reshape(dirs, faces, 1, length),
        warm_start.reshape(dirs, faces, 1, length),
        inverse_blocks.reshape(faces, length, length),
        coarse_basis.reshape(modes, faces, 1, length),
        mortar_rows.reshape(rows, length),
        slave_owner.reshape(1, rows),
        slave_dofs.reshape(1, rows),
        active_set.reshape(1, rows),
        match_rounds.reshape(1, N_MATCH),
        row_counts.reshape(1, 1),
    )
    return result.reshape(dirs, 1, 1, faces, length)


def solution(mesh):
    in_specs = (
        P(None, "organ", "sub", None, None),
        P(None, "organ", "sub", None, None),
        P("organ", "sub", None, None, None),
        P(None, "organ", "sub", None, None),
        P("organ", "sub", None, None),
        P("organ", "sub", None),
        P("organ", "sub", None, None),
        P("organ", "sub", None),
        P("organ", "sub", None),
        P("organ", "sub", None),
    )
    out_specs = P(None, "organ", "sub", None, None)
    return jax.shard_map(local, mesh=mesh, in_specs=in_specs, out_specs=out_specs, check_vma=False)
```
